128 devices in a mesh: frames: 2 (over core), pix: 64 (over z, y, x).
Axes of the slice: x: 4, y: 4, z: 4, core: 2. Of those that a mesh axis runs over, the one named last changes fastest.
Arguments:
- frames: float32 [256, 32768], P('frames', 'pix'), may hold values from -6 to 6
Outputs:
- sketch: float32 [128, 32768], P(None, 'pix')
- projected: float32 [256, 32768], P('frames', 'pix')
The draws below stay inside these ranges and needn't reach their ends.
All inputs are finite; a program needn't handle non-finite values.
Results may differ from the reference program's by a relative error of at most 0.0003.
Values sent between devices are 32-bit elements; how exact they have to be, the bound alone decides.
A program may use at most 64 MiB of HBM per device.

```python
import jax
import jax.numpy as jnp
from jax import lax

ELL = 128
PIX = 32768
POWER = 1
FRAMES = 256
LEVELS = 1
N_FRAMES = 2


def shard_levels(own_key, dims, split, least, top_value):
    gain = 1.0
    for dim, blocks in split:
        draws = jax.random.uniform(jax.random.fold_in(jax.random.fold_in(own_key, 6), dim), (blocks,), jnp.float32, least / len(split), top_value / len(split))
        gain = gain * jnp.repeat(jnp.exp(draws), dims[dim] // blocks).reshape((-1,) + (1,) * (len(dims) - 1 - dim))
    return gain


def noise(own_key, extent, spread, reach, split=(), kind=jnp.bfloat16):
    array = spread * jax.random.normal(own_key, extent, jnp.float32)
    if split:
        array = array * shard_levels(own_key, extent, split, -0.22, 0.18)
    return jnp.clip(array, -reach, reach).astype(kind)


def setup_inputs(seed: int = 0) -> dict:
    key_of = jax.random.split(jax.random.key(seed), 2)
    return {
        "frames": noise(key_of[0], (FRAMES, PIX), 1.0, 6.0, ((0, 2), (1, 64)), jnp.float32),
    }


def hdot(left, right):
    return jnp.dot(left.astype(jnp.float32), right.astype(jnp.float32), precision=lax.Precision.HIGHEST, preferred_element_type=jnp.float32)

def lower_solve(factor, rhs):
    return lax.linalg.triangular_solve(factor, rhs, left_side=True, lower=True)

def rotation(stacked_gram):
    kept = stacked_gram.shape[0] // 2
    subspace = jnp.eye(2 * kept, kept, dtype=jnp.float32)
    for _ in range(POWER):
        product = hdot(stacked_gram, subspace)
        factor = jnp.linalg.cholesky(hdot(product.T, product))
        subspace = lower_solve(factor, product.T).T
    reduced = hdot(subspace.T, hdot(stacked_gram, subspace))
    root_factor = jnp.linalg.cholesky(reduced)
    delta = jnp.trace(reduced) / kept
    damped = jnp.linalg.cholesky(reduced + delta * jnp.eye(kept, dtype=jnp.float32))
    shrunk = lower_solve(damped, reduced)
    whitened = lower_solve(root_factor, subspace.T)
    mixing = hdot(shrunk.T, whitened)
    return (mixing, hdot(shrunk.T, shrunk))

def merge_pair(lower_rows, lower_gram, upper_rows, upper_gram):
    kept = lower_rows.shape[0]
    cross = hdot(lower_rows, upper_rows.T)
    stacked_gram = jnp.concatenate([jnp.concatenate([lower_gram, cross], axis=1), jnp.concatenate([cross.T, upper_gram], axis=1)], axis=0)
    mixing, new_gram = rotation(stacked_gram)
    merged = hdot(mixing[:, :kept], lower_rows) + hdot(mixing[:, kept:], upper_rows)
    return (merged, new_gram)

def reference(frames):
    sketches = frames.reshape(N_FRAMES, ELL, PIX)
    grams = jax.vmap(lambda rows: hdot(rows, rows.T))(sketches)
    for _ in range(LEVELS):
        sketches, grams = jax.vmap(merge_pair)(sketches[0::2], grams[0::2], sketches[1::2], grams[1::2])
    sketch = sketches[0]
    root_gram = grams[0]
    coeffs = hdot(frames, sketch.T)
    scaling = 4.0 * ELL / (jnp.trace(root_gram) + 1e-06)
    projected = hdot(coeffs, sketch) * scaling
    return (sketch, projected)
```

```python
import functools
import jax
import jax.numpy as jnp
from jax import lax
from jax.experimental import pallas as pl
from jax.experimental.pallas import tpu as pltpu
from jax.sharding import PartitionSpec as P

MESH = pl.DeviceIdType.MESH
HI = lax.Precision.HIGHEST
F32 = jnp.float32


def mm(a, b, ca=1, cb=0, prec=HI):
    return lax.dot_general(a, b, (((ca,), (cb,)), ((), ())), precision=prec, preferred_element_type=jnp.float32)

def inverse_factors(mats, PW=32, IB=16):
    n = 128
    lane = lax.broadcasted_iota(jnp.int32, (8, n), 1)
    sub = lax.broadcasted_iota(jnp.int32, (8, n), 0)
    nb = n // 8
    X = [[m[8 * i:8 * i + 8] for i in range(nb)] for m in mats]
    for r0 in range(0, n, PW):
        b0, b1 = r0 // 8, (r0 + PW) // 8
        D = [[None] * nb for _ in mats]
        for i0 in range(r0, r0 + PW, IB):
            ib = i0 // 8
            inner = (lane >= i0) & (lane < i0 + IB)
            CB = [[[None] * nb for _ in range(IB)] for _ in mats]
            for q in range(len(mats)):
                for k in range(IB):
                    for b in range((i0 + k) // 8, b1):
                        CB[q][k][b] = jnp.broadcast_to(X[q][b][:, i0 + k:i0 + k + 1], (8, n))
                for b in range(ib, b1):
                    X[q][b] = jnp.where(inner, jnp.where(lane == sub + 8 * b, 1.0, 0.0), X[q][b])
            for j in range(IB):
                row = i0 + j
                jb, js = row // 8, row % 8
                for q in range(len(mats)):
                    c = CB[q][j]
                    piv = jnp.broadcast_to(c[jb][js:js + 1], (8, n))
                    D[q][jb] = piv if D[q][jb] is None else jnp.where(sub >= js, piv, D[q][jb])
                    r = 1.0 / piv
                    xrow = jnp.broadcast_to(X[q][jb][js:js + 1], (8, n)) * r
                    for k in range(j + 1, IB):
                        kr = i0 + k
                        s = jnp.broadcast_to(c[kr // 8][kr % 8:kr % 8 + 1], (8, n)) * r
                        for b in range(kr // 8, b1):
                            CB[q][k][b] = CB[q][k][b] - c[b] * s
                    for b in range(jb, b1):
                        if b == jb:
                            if js == 7: continue
                            X[q][b] = X[q][b] - jnp.where(sub > js, c[b], 0.0) * xrow
                        else:
                            X[q][b] = X[q][b] - c[b] * xrow
        for q in range(len(mats)):
            for b in range(b0, b1):
                X[q][b] = X[q][b] * lax.rsqrt(D[q][b])
                if IB < PW:
                    X[q][b] = jnp.where((lane > sub + 8 * b) & (lane < r0 + PW), 0.0, X[q][b])
            if b1 < nb:
                U = jnp.concatenate(X[q][b0:b1], axis=0)
                upd = mm(U[:, r0 + PW:], U, 0, 0) if (r0 + PW) % 128 == 0 else mm(U, U, 0, 0)
                off = b1 if upd.shape[0] == n else 0
                panel = (lane >= r0) & (lane < r0 + PW)
                for b in range(b1, nb):
                    X[q][b] = jnp.where(panel, 0.0, X[q][b]) - upd[8 * b:8 * b + 8]
    out = []
    for q in range(len(mats)):
        out.append(jnp.concatenate([jnp.where(lane <= sub + 8 * b, X[q][b], 0.0) for b in range(nb)], axis=0))
    return out

def k2(core_of, opts, gk, gc, stack, sketch_ref, proj_ref):
    core = core_of()
    n = 128
    Ka = gk[0:16].reshape(n, n); Kb = gk[16:32].reshape(n, n); C = gc[...].reshape(n, n)
    N = mm(Ka, Ka) + mm(C, C, 1, 1)
    (Finv,) = inverse_factors([N], **opts)
    Va = mm(Finv, Ka); Vb = mm(Finv, C)
    Ct = C.T
    Ga = mm(Va, Ka) + mm(Vb, Ct)
    Gb = mm(Va, C) + mm(Vb, Kb)
    Hm = mm(Ga, Va, 1, 1) + mm(Gb, Vb, 1, 1)
    ii = lax.broadcasted_iota(jnp.int32, (n, n), 0); jj = lax.broadcasted_iota(jnp.int32, (n, n), 1)
    eye = jnp.where(ii == jj, 1.0, 0.0)
    delta = jnp.sum(Hm * eye, keepdims=True) * (1.0 / n)
    Rinv, Linv = inverse_factors([Hm, Hm + delta * eye], **opts)
    Pm = mm(Linv, Hm)
    Wa = mm(Rinv, Va); Wb = mm(Rinv, Vb)
    Ma = mm(Pm, Wa, 0, 0); Mb = mm(Pm, Wb, 0, 0)
    scale = (4.0 * n) / (jnp.sum(Pm * Pm, keepdims=True) + 1e-06)
    sk = mm(Ma, stack[0]) + mm(Mb, stack[1])
    sketch_ref[...] = sk
    up = core == 1
    L = jnp.where(up, Ct, Ka); R = jnp.where(up, Kb, C)
    co = mm(L, Ma, 1, 1) + mm(R, Mb, 1, 1)
    proj_ref[...] = mm(co * scale, sk)

def call_k2(gk, gc, stack, core_of=lambda: lax.axis_index("frames"), opts=dict(PW=32, IB=16), name="merge_project"):
    V = pl.BlockSpec(memory_space=pltpu.VMEM)
    o = jax.ShapeDtypeStruct((128, 512), jnp.float32)
    return pl.pallas_call(functools.partial(k2, core_of, opts), out_shape=[o, o], in_specs=[V] * 3, out_specs=[V] * 2,
        compiler_params=pltpu.CompilerParams(vmem_limit_bytes=32 << 20), name=name)(gk, gc, stack)


def tree(buf, own, count):
    v = [own] + [buf[d] for d in range(1, count)]
    while len(v) > 1:
        v = [v[i] + v[i + 1] for i in range(0, len(v), 2)]
    return v[0]


def k1(fr, gk, gc, stack, kown, cown, rk, rc, sk, sc, zk, zc, s_ex, r_ex, s_rs, r_rs, s_z, r_z, s_ag, r_ag):
    core = lax.axis_index("frames")
    pix = lax.axis_index("pix")
    z = pix // 16
    p = pix % 16
    bar = pltpu.get_barrier_semaphore()
    greeted = 0
    for d in range(16):
        for e in range(2):
            if d or e:
                pl.semaphore_signal(bar, inc=1, device_id=((core + e) % 2, z * 16 + (p ^ d)), device_id_type=MESH)
                greeted += 1
    for d in range(1, 4):
        pl.semaphore_signal(bar, inc=1, device_id=(core, (z ^ d) * 16 + p), device_id_type=MESH)
        greeted += 1

    def rcopy(src, dst, ss, rs, c, q):
        return pltpu.make_async_remote_copy(src_ref=src, dst_ref=dst, send_sem=ss, recv_sem=rs, device_id=(c, q), device_id_type=MESH)

    mine = fr[...]
    kown[...] = mm(mine, mine, 1, 1).reshape(16, 8, 128)
    stack[core] = mine
    pl.semaphore_wait(bar, greeted)
    ex = rcopy(stack.at[core], stack.at[core], s_ex, r_ex, (core + 1) % 2, pix)
    ex.start()
    for d in range(1, 16):
        rcopy(kown.at[p ^ d], rk.at[d], s_rs.at[0], r_rs.at[0], core, z * 16 + (p ^ d)).start()
    ex.wait()
    half = pl.multiple_of(core * 64, 64)
    cown[...] = mm(stack[0, pl.ds(half, 64), :], stack[1], 1, 1).reshape(16, 4, 128)
    for d in range(1, 16):
        rcopy(cown.at[p ^ d], rc.at[d], s_rs.at[1], r_rs.at[1], core, z * 16 + (p ^ d)).start()

    def wait_for(out, into, ss, rs, count):
        rcopy(out.at[pl.ds(0, count)], into.at[pl.ds(0, count)], ss, rs, (core + 1) % 2, pix).wait()

    wait_for(kown, rk, s_rs.at[0], r_rs.at[0], 15)
    sk[...] = tree(rk, kown[p], 16)
    for d in range(1, 4):
        rcopy(sk, zk.at[d], s_z.at[0], r_z.at[0], core, (z ^ d) * 16 + p).start()
    wait_for(cown, rc, s_rs.at[1], r_rs.at[1], 15)
    sc[...] = tree(rc, cown[p], 16)
    for d in range(1, 4):
        rcopy(sc, zc.at[d], s_z.at[1], r_z.at[1], core, (z ^ d) * 16 + p).start()
    wait_for(kown, zk, s_z.at[0], r_z.at[0], 3)
    gk[core * 16 + p] = tree(zk, sk[...], 4)
    for d in range(16):
        for e in range(2):
            if d or e:
                rcopy(gk.at[core * 16 + p], gk.at[core * 16 + p], s_ag.at[0], r_ag.at[0], (core + e) % 2, z * 16 + (p ^ d)).start()
    wait_for(cown, zc, s_z.at[1], r_z.at[1], 3)
    gc[core * 16 + p] = tree(zc, sc[...], 4)
    for d in range(16):
        for e in range(2):
            if d or e:
                rcopy(gc.at[core * 16 + p], gc.at[core * 16 + p], s_ag.at[1], r_ag.at[1], (core + e) % 2, z * 16 + (p ^ d)).start()
    for i, g in enumerate((gk, gc)):
        wait_for(g, g, s_ag.at[i], r_ag.at[i], 31)


def call_k1(frames):
    vm = pl.BlockSpec(memory_space=pltpu.VMEM)
    dma = pltpu.SemaphoreType.DMA
    return pl.pallas_call(
        k1,
        out_shape=[
            jax.ShapeDtypeStruct((32, 8, 128), F32),
            jax.ShapeDtypeStruct((32, 4, 128), F32),
            jax.ShapeDtypeStruct((2, 128, 512), F32),
        ],
        in_specs=[vm],
        out_specs=[vm] * 3,
        scratch_shapes=[
            pltpu.VMEM((16, 8, 128), F32),
            pltpu.VMEM((16, 4, 128), F32),
            pltpu.VMEM((16, 8, 128), F32),
            pltpu.VMEM((16, 4, 128), F32),
            pltpu.VMEM((8, 128), F32),
            pltpu.VMEM((4, 128), F32),
            pltpu.VMEM((4, 8, 128), F32),
            pltpu.VMEM((4, 4, 128), F32),
            dma(()), dma(()), dma((2,)), dma((2,)), dma((2,)), dma((2,)), dma((2,)), dma((2,)),
        ],
        compiler_params=pltpu.CompilerParams(collective_id=0, has_side_effects=True, vmem_limit_bytes=32 << 20),
        name="gram_exchange",
    )(frames)


def local(frames):
    gk, gc, stack = call_k1(frames)
    return tuple(call_k2(gk, gc, stack))


def solution(mesh):
    return jax.shard_map(
        local,
        mesh=mesh,
        in_specs=(P("frames", "pix"),),
        out_specs=(P(None, "pix"), P("frames", "pix")),
        check_vma=False,
    )
```

```python
import functools
import jax
import jax.numpy as jnp
from jax import lax
from jax.experimental import pallas as pl
from jax.experimental.pallas import tpu as pltpu
from jax.sharding import PartitionSpec as P

MESH = pl.DeviceIdType.MESH
HI = lax.Precision.HIGHEST
F32 = jnp.float32


def mm(a, b, ca=1, cb=0, prec=HI):
    return lax.dot_general(a, b, (((ca,), (cb,)), ((), ())), precision=prec, preferred_element_type=jnp.float32)

def inverse_factors(mats, PW=32, IB=16):
    n = 128
    lane = lax.broadcasted_iota(jnp.int32, (8, n), 1)
    sub = lax.broadcasted_iota(jnp.int32, (8, n), 0)
    nb = n // 8
    X = [[m[8 * i:8 * i + 8] for i in range(nb)] for m in mats]
    for r0 in range(0, n, PW):
        b0, b1 = r0 // 8, (r0 + PW) // 8
        D = [[None] * nb for _ in mats]
        for i0 in range(r0, r0 + PW, IB):
            ib = i0 // 8
            inner = (lane >= i0) & (lane < i0 + IB)
            CB = [[[None] * nb for _ in range(IB)] for _ in mats]
            for q in range(len(mats)):
                for k in range(IB):
                    for b in range((i0 + k) // 8, b1):
                        CB[q][k][b] = jnp.broadcast_to(X[q][b][:, i0 + k:i0 + k + 1], (8, n))
                for b in range(ib, b1):
                    X[q][b] = jnp.where(inner, jnp.where(lane == sub + 8 * b, 1.0, 0.0), X[q][b])
            for j in range(IB):
                row = i0 + j
                jb, js = row // 8, row % 8
                for q in range(len(mats)):
                    c = CB[q][j]
                    piv = jnp.broadcast_to(c[jb][js:js + 1], (8, n))
                    D[q][jb] = piv if D[q][jb] is None else jnp.where(sub >= js, piv, D[q][jb])
                    r = 1.0 / piv
                    xrow = jnp.broadcast_to(X[q][jb][js:js + 1], (8, n)) * r
                    for k in range(j + 1, IB):
                        kr = i0 + k
                        s = jnp.broadcast_to(c[kr // 8][kr % 8:kr % 8 + 1], (8, n)) * r
                        for b in range(kr // 8, b1):
                            CB[q][k][b] = CB[q][k][b] - c[b] * s
                    for b in range(jb, b1):
                        if b == jb:
                            if js == 7: continue
                            X[q][b] = X[q][b] - jnp.where(sub > js, c[b], 0.0) * xrow
                        else:
                            X[q][b] = X[q][b] - c[b] * xrow
        for q in range(len(mats)):
            for b in range(b0, b1):
                X[q][b] = X[q][b] * lax.rsqrt(D[q][b])
                if IB < PW:
                    X[q][b] = jnp.where((lane > sub + 8 * b) & (lane < r0 + PW), 0.0, X[q][b])
            if b1 < nb:
                U = jnp.concatenate(X[q][b0:b1], axis=0)
                upd = mm(U[:, r0 + PW:], U, 0, 0) if (r0 + PW) % 128 == 0 else mm(U, U, 0, 0)
                off = b1 if upd.shape[0] == n else 0
                panel = (lane >= r0) & (lane < r0 + PW)
                for b in range(b1, nb):
                    X[q][b] = jnp.where(panel, 0.0, X[q][b]) - upd[8 * b:8 * b + 8]
    out = []
    for q in range(len(mats)):
        out.append(jnp.concatenate([jnp.where(lane <= sub + 8 * b, X[q][b], 0.0) for b in range(nb)], axis=0))
    return out

def k2(core_of, opts, gk, gc, stack, sketch_ref, proj_ref):
    core = core_of()
    n = 128
    Ka = gk[0:8].reshape(n, n); Kb = gk[8:16].reshape(n, n); C = gc[...].reshape(n, n)
    N = mm(Ka, Ka) + mm(C, C, 1, 1)
    (Finv,) = inverse_factors([N], **opts)
    Va = mm(Finv, Ka); Vb = mm(Finv, C)
    Ct = C.T
    Ga = mm(Va, Ka) + mm(Vb, Ct)
    Gb = mm(Va, C) + mm(Vb, Kb)
    Hm = mm(Ga, Va, 1, 1) + mm(Gb, Vb, 1, 1)
    ii = lax.broadcasted_iota(jnp.int32, (n, n), 0); jj = lax.broadcasted_iota(jnp.int32, (n, n), 1)
    eye = jnp.where(ii == jj, 1.0, 0.0)
    delta = jnp.sum(Hm * eye, keepdims=True) * (1.0 / n)
    Rinv, Linv = inverse_factors([Hm, Hm + delta * eye], **opts)
    Pm = mm(Linv, Hm)
    Wa = mm(Rinv, Va); Wb = mm(Rinv, Vb)
    Ma = mm(Pm, Wa, 0, 0); Mb = mm(Pm, Wb, 0, 0)
    scale = (4.0 * n) / (jnp.sum(Pm * Pm, keepdims=True) + 1e-06)
    sk = mm(Ma, stack[0]) + mm(Mb, stack[1])
    sketch_ref[...] = sk
    up = core == 1
    L = jnp.where(up, Ct, Ka); R = jnp.where(up, Kb, C)
    co = mm(L, Ma, 1, 1) + mm(R, Mb, 1, 1)
    proj_ref[...] = mm(co * scale, sk)

def call_k2(gk, gc, stack, core_of=lambda: lax.axis_index("frames"), opts=dict(PW=32, IB=16), name="merge_project"):
    V = pl.BlockSpec(memory_space=pltpu.VMEM)
    o = jax.ShapeDtypeStruct((128, 512), jnp.float32)
    return pl.pallas_call(functools.partial(k2, core_of, opts), out_shape=[o, o], in_specs=[V] * 3, out_specs=[V] * 2,
        compiler_params=pltpu.CompilerParams(vmem_limit_bytes=32 << 20), name=name)(gk, gc, stack)


def tree(buf, own):
    v = [own] + [buf[e] for e in range(1, 8)]
    while len(v) > 1:
        v = [v[i] + v[i + 1] for i in range(0, len(v), 2)]
    return v[0]


NEAR = (7, 6, 5, 3, 4, 2, 1)


def step(e, unit):
    return unit * ((e & 1) + 4 * (e >> 1 & 1) + 16 * (e >> 2))


def k1(hbm, gk, gc, stack, kown, cown, rk, rc, sk, sc, zk, zc, s_in, s_ex, r_ex, s_rs, r_rs, s_z, r_z, s_ag, r_ag):
    core = lax.axis_index("frames")
    pix = lax.axis_index("pix")
    partner = (core + 1) % 2
    load = pltpu.make_async_copy(hbm, stack.at[core], s_in)
    load.start()
    bit = lambda t: (t % 4 + 1) // 2 % 2
    own = bit(pix) + 2 * bit(pix // 4) + 4 * bit(pix // 16)
    mates = [((core + f) % 2, pix ^ step(e, 1)) for e in NEAR + (0,) for f in (0, 1) if e or f]
    others = [(core, pix ^ step(e, 3)) for e in NEAR]
    bar = pltpu.get_barrier_semaphore()
    for device in others + mates:
        pl.semaphore_signal(bar, inc=1, device_id=device, device_id_type=MESH)

    def rcopy(src, dst, ss, rs, device):
        return pltpu.make_async_remote_copy(src_ref=src, dst_ref=dst, send_sem=ss, recv_sem=rs, device_id=device, device_id_type=MESH)

    load.wait()
    mine = stack[core]
    kown[...] = mm(mine, mine, 1, 1).reshape(8, 16, 128)
    pl.semaphore_wait(bar, len(others + mates))
    ex = rcopy(stack.at[core], stack.at[core], s_ex, r_ex, (partner, pix))
    ex.start()

    def scatter(block, into, i):
        for e in NEAR:
            rcopy(block.at[own ^ e], into.at[e], s_rs.at[i], r_rs.at[i], (core, pix ^ step(e, 1))).start()

    def across(block, into, i):
        for e in NEAR:
            rcopy(block, into.at[e], s_z.at[i], r_z.at[i], (core, pix ^ step(e, 3))).start()

    def gather(g, i):
        for device in mates:
            rcopy(g.at[core * 8 + own], g.at[core * 8 + own], s_ag.at[i], r_ag.at[i], device).start()

    def wait_for(buf, ss, rs, count):
        some = buf.at[pl.ds(0, count)]
        rcopy(some, some, ss, rs, (partner, pix)).wait()

    scatter(kown, rk, 0)
    ex.wait()
    half = pl.multiple_of(core * 64, 64)
    cown[...] = mm(stack[0, pl.ds(half, 64), :], stack[1], 1, 1).reshape(8, 8, 128)
    scatter(cown, rc, 1)
    wait_for(rk, s_rs.at[0], r_rs.at[0], 7)
    sk[...] = tree(rk, kown[own])
    across(sk, zk, 0)
    wait_for(rc, s_rs.at[1], r_rs.at[1], 7)
    sc[...] = tree(rc, cown[own])
    across(sc, zc, 1)
    wait_for(zk, s_z.at[0], r_z.at[0], 7)
    gk[core * 8 + own] = tree(zk, sk[...])
    gather(gk, 0)
    wait_for(zc, s_z.at[1], r_z.at[1], 7)
    gc[core * 8 + own] = tree(zc, sc[...])
    gather(gc, 1)
    wait_for(gk, s_ag.at[0], r_ag.at[0], 15)
    wait_for(gc, s_ag.at[1], r_ag.at[1], 15)


def call_k1(frames):
    vm = pl.BlockSpec(memory_space=pltpu.VMEM)
    dma = pltpu.SemaphoreType.DMA
    return pl.pallas_call(
        k1,
        out_shape=[
            jax.ShapeDtypeStruct((16, 16, 128), F32),
            jax.ShapeDtypeStruct((16, 8, 128), F32),
            jax.ShapeDtypeStruct((2, 128, 512), F32),
        ],
        in_specs=[pl.BlockSpec(memory_space=pltpu.HBM)],
        out_specs=[vm] * 3,
        scratch_shapes=[
            pltpu.VMEM((8, 16, 128), F32),
            pltpu.VMEM((8, 8, 128), F32),
            pltpu.VMEM((8, 16, 128), F32),
            pltpu.VMEM((8, 8, 128), F32),
            pltpu.VMEM((16, 128), F32),
            pltpu.VMEM((8, 128), F32),
            pltpu.VMEM((8, 16, 128), F32),
            pltpu.VMEM((8, 8, 128), F32),
            dma(()), dma(()), dma(()), dma((2,)), dma((2,)), dma((2,)), dma((2,)), dma((2,)), dma((2,)),
        ],
        compiler_params=pltpu.CompilerParams(collective_id=0, has_side_effects=True, vmem_limit_bytes=32 << 20),
        name="gram_exchange",
    )(frames)


def local(frames):
    gk, gc, stack = call_k1(pltpu.with_memory_space_constraint(frames, pltpu.HBM))
    return tuple(call_k2(gk, gc, stack))


def solution(mesh):
    return jax.shard_map(
        local,
        mesh=mesh,
        in_specs=(P("frames", "pix"),),
        out_specs=(P(None, "pix"), P("frames", "pix")),
        check_vma=False,
    )
```

```python
import functools
import jax
import jax.numpy as jnp
from jax import lax
from jax.experimental import pallas as pl
from jax.experimental.pallas import tpu as pltpu
from jax.sharding import PartitionSpec as P

MESH = pl.DeviceIdType.MESH
HI = lax.Precision.HIGHEST
F32 = jnp.float32


def mm(a, b, ca=1, cb=0, prec=HI):
    return lax.dot_general(a, b, (((ca,), (cb,)), ((), ())), precision=prec, preferred_element_type=jnp.float32)

def inverse_factors(mats, PW=32, IB=16):
    n = 128
    lane = lax.broadcasted_iota(jnp.int32, (8, n), 1)
    sub = lax.broadcasted_iota(jnp.int32, (8, n), 0)
    nb = n // 8
    X = [[m[8 * i:8 * i + 8] for i in range(nb)] for m in mats]
    for r0 in range(0, n, PW):
        b0, b1 = r0 // 8, (r0 + PW) // 8
        D = [[None] * nb for _ in mats]
        for i0 in range(r0, r0 + PW, IB):
            ib = i0 // 8
            inner = (lane >= i0) & (lane < i0 + IB)
            CB = [[[None] * nb for _ in range(IB)] for _ in mats]
            for q in range(len(mats)):
                for k in range(IB):
                    for b in range((i0 + k) // 8, b1):
                        CB[q][k][b] = jnp.broadcast_to(X[q][b][:, i0 + k:i0 + k + 1], (8, n))
                for b in range(ib, b1):
                    X[q][b] = jnp.where(inner, jnp.where(lane == sub + 8 * b, 1.0, 0.0), X[q][b])
            for j in range(IB):
                row = i0 + j
                jb, js = row // 8, row % 8
                for q in range(len(mats)):
                    c = CB[q][j]
                    piv = jnp.broadcast_to(c[jb][js:js + 1], (8, n))
                    D[q][jb] = piv if D[q][jb] is None else jnp.where(sub >= js, piv, D[q][jb])
                    r = 1.0 / piv
                    xrow = jnp.broadcast_to(X[q][jb][js:js + 1], (8, n)) * r
                    for k in range(j + 1, IB):
                        kr = i0 + k
                        s = jnp.broadcast_to(c[kr // 8][kr % 8:kr % 8 + 1], (8, n)) * r
                        for b in range(kr // 8, b1):
                            CB[q][k][b] = CB[q][k][b] - c[b] * s
                    for b in range(jb, b1):
                        if b == jb:
                            if js == 7: continue
                            X[q][b] = X[q][b] - jnp.where(sub > js, c[b], 0.0) * xrow
                        else:
                            X[q][b] = X[q][b] - c[b] * xrow
        for q in range(len(mats)):
            for b in range(b0, b1):
                X[q][b] = X[q][b] * lax.rsqrt(D[q][b])
                if IB < PW:
                    X[q][b] = jnp.where((lane > sub + 8 * b) & (lane < r0 + PW), 0.0, X[q][b])
            if b1 < nb:
                U = jnp.concatenate(X[q][b0:b1], axis=0)
                upd = mm(U[:, r0 + PW:], U, 0, 0) if (r0 + PW) % 128 == 0 else mm(U, U, 0, 0)
                off = b1 if upd.shape[0] == n else 0
                panel = (lane >= r0) & (lane < r0 + PW)
                for b in range(b1, nb):
                    X[q][b] = jnp.where(panel, 0.0, X[q][b]) - upd[8 * b:8 * b + 8]
    out = []
    for q in range(len(mats)):
        out.append(jnp.concatenate([jnp.where(lane <= sub + 8 * b, X[q][b], 0.0) for b in range(nb)], axis=0))
    return out

def k2(core_of, opts, gk, gc, stack, sketch_hbm, proj_hbm, sketch, proj, sem):
    core = core_of()
    n = 128
    Ka = gk[0:8].reshape(n, n)
    Kb = gk[8:16].reshape(n, n)
    C = gc[...].reshape(n, n)
    WT = jnp.concatenate([Ka, C], axis=1)
    N = mm(WT, WT, 1, 1)
    Z = mm(WT, jnp.concatenate([WT, jnp.concatenate([C.T, Kb], axis=1)], axis=0))
    (Finv,) = inverse_factors([N], **opts)
    VT = mm(Finv, WT)
    VG = mm(Finv, Z)
    H = mm(VG, VT, 1, 1)
    delta = jnp.sum(jnp.sum(VG * VT, axis=0, keepdims=True), axis=1, keepdims=True) * (1.0 / n)
    ii = lax.broadcasted_iota(jnp.int32, (n, n), 0)
    jj = lax.broadcasted_iota(jnp.int32, (n, n), 1)
    VF = mm(VT, stack[...].reshape(2 * n, stack.shape[2]))
    GV = jnp.where(core == 1, VG[:, n:], VG[:, :n]).T
    Rinv, Linv = inverse_factors([H, H + jnp.where(ii == jj, delta, 0.0)], **opts)
    WF = mm(Rinv, VF)
    PT = mm(H, Linv, 1, 1)
    Pm = mm(Linv, H)
    YT = mm(GV, Rinv, 1, 1)
    sk = mm(PT, WF)
    sketch[...] = sk
    out = pltpu.make_async_copy(sketch, sketch_hbm, sem.at[0])
    out.start()
    co = mm(YT, Pm)
    gram_trace = jnp.sum(jnp.sum(Pm * Pm, axis=0, keepdims=True), axis=1, keepdims=True)
    proj[...] = mm(co * ((4.0 * n) / (gram_trace + 1e-06)), sk)
    last = pltpu.make_async_copy(proj, proj_hbm, sem.at[1])
    last.start()
    out.wait()
    last.wait()


def call_k2(gk, gc, stack, core_of=lambda: lax.axis_index("frames"), opts=dict(PW=32, IB=16), name="merge_project"):
    V = pl.BlockSpec(memory_space=pltpu.VMEM)
    o = jax.ShapeDtypeStruct((128, 512), jnp.float32)
    return pl.pallas_call(functools.partial(k2, core_of, opts), out_shape=[o, o], in_specs=[V] * 3, out_specs=[pl.BlockSpec(memory_space=pltpu.HBM)] * 2,
        scratch_shapes=[pltpu.VMEM((128, 512), jnp.float32)] * 2 + [pltpu.SemaphoreType.DMA((2,))],
        compiler_params=pltpu.CompilerParams(vmem_limit_bytes=32 << 20), name=name)(gk, gc, stack)


def tree(buf, own):
    v = [own] + [buf[e] for e in range(1, 8)]
    while len(v) > 1:
        v = [v[i] + v[i + 1] for i in range(0, len(v), 2)]
    return v[0]


NEAR = (7, 6, 5, 3, 4, 2, 1)


def step(e, unit):
    return unit * ((e & 1) + 4 * (e >> 1 & 1) + 16 * (e >> 2))


def k1(hbm, gk, gc, stack, kown, cown, rk, rc, sk, sc, zk, zc, s_in, s_ex, r_ex, s_rs, r_rs, s_z, r_z, s_ag, r_ag):
    core = lax.axis_index("frames")
    pix = lax.axis_index("pix")
    partner = (core + 1) % 2
    load = pltpu.make_async_copy(hbm, stack.at[core], s_in)
    load.start()
    bit = lambda t: (t % 4 + 1) // 2 % 2
    own = bit(pix) + 2 * bit(pix // 4) + 4 * bit(pix // 16)
    mates = [((core + f) % 2, pix ^ step(e, 1)) for e in NEAR + (0,) for f in (0, 1) if e or f]
    others = [(core, pix ^ step(e, 3)) for e in NEAR]
    bar = pltpu.get_barrier_semaphore()
    for device in others + mates:
        pl.semaphore_signal(bar, inc=1, device_id=device, device_id_type=MESH)

    def rcopy(src, dst, ss, rs, device):
        return pltpu.make_async_remote_copy(src_ref=src, dst_ref=dst, send_sem=ss, recv_sem=rs, device_id=device, device_id_type=MESH)

    load.wait()
    mine = stack[core]
    kown[...] = mm(mine, mine, 1, 1).reshape(8, 16, 128)
    pl.semaphore_wait(bar, len(others + mates))
    ex = rcopy(stack.at[core], stack.at[core], s_ex, r_ex, (partner, pix))
    ex.start()

    def scatter(block, into, i):
        for e in NEAR:
            rcopy(block.at[own ^ e], into.at[e], s_rs.at[i], r_rs.at[i], (core, pix ^ step(e, 1))).start()

    def across(block, into, i):
        for e in NEAR:
            rcopy(block, into.at[e], s_z.at[i], r_z.at[i], (core, pix ^ step(e, 3))).start()

    def gather(g, i):
        for device in mates:
            rcopy(g.at[core * 8 + own], g.at[core * 8 + own], s_ag.at[i], r_ag.at[i], device).start()

    def wait_for(buf, ss, rs, count):
        some = buf.at[pl.ds(0, count)]
        rcopy(some, some, ss, rs, (partner, pix)).wait()

    scatter(kown, rk, 0)
    ex.wait()
    half = pl.multiple_of(core * 64, 64)
    cown[...] = mm(stack[0, pl.ds(half, 64), :], stack[1], 1, 1).reshape(8, 8, 128)
    scatter(cown, rc, 1)
    wait_for(rk, s_rs.at[0], r_rs.at[0], 7)
    sk[...] = tree(rk, kown[own])
    across(sk, zk, 0)
    wait_for(rc, s_rs.at[1], r_rs.at[1], 7)
    sc[...] = tree(rc, cown[own])
    across(sc, zc, 1)
    wait_for(zk, s_z.at[0], r_z.at[0], 7)
    gk[core * 8 + own] = tree(zk, sk[...])
    gather(gk, 0)
    wait_for(zc, s_z.at[1], r_z.at[1], 7)
    gc[core * 8 + own] = tree(zc, sc[...])
    gather(gc, 1)
    wait_for(gk, s_ag.at[0], r_ag.at[0], 15)
    wait_for(gc, s_ag.at[1], r_ag.at[1], 15)


def call_k1(frames):
    vm = pl.BlockSpec(memory_space=pltpu.VMEM)
    dma = pltpu.SemaphoreType.DMA
    return pl.pallas_call(
        k1,
        out_shape=[
            jax.ShapeDtypeStruct((16, 16, 128), F32),
            jax.ShapeDtypeStruct((16, 8, 128), F32),
            jax.ShapeDtypeStruct((2, 128, 512), F32),
        ],
        in_specs=[pl.BlockSpec(memory_space=pltpu.HBM)],
        out_specs=[vm] * 3,
        scratch_shapes=[
            pltpu.VMEM((8, 16, 128), F32),
            pltpu.VMEM((8, 8, 128), F32),
            pltpu.VMEM((8, 16, 128), F32),
            pltpu.VMEM((8, 8, 128), F32),
            pltpu.VMEM((16, 128), F32),
            pltpu.VMEM((8, 128), F32),
            pltpu.VMEM((8, 16, 128), F32),
            pltpu.VMEM((8, 8, 128), F32),
            dma(()), dma(()), dma(()), dma((2,)), dma((2,)), dma((2,)), dma((2,)), dma((2,)), dma((2,)),
        ],
        compiler_params=pltpu.CompilerParams(collective_id=0, has_side_effects=True, vmem_limit_bytes=32 << 20),
        name="gram_exchange",
    )(frames)


def local(frames):
    gk, gc, stack = call_k1(pltpu.with_memory_space_constraint(frames, pltpu.HBM))
    return tuple(call_k2(gk, gc, stack))


def solution(mesh):
    return jax.shard_map(
        local,
        mesh=mesh,
        in_specs=(P("frames", "pix"),),
        out_specs=(P(None, "pix"), P("frames", "pix")),
        check_vma=False,
    )
```

```python
import functools
import jax
import jax.numpy as jnp
from jax import lax
from jax.experimental import pallas as pl
from jax.experimental.pallas import tpu as pltpu
from jax.sharding import PartitionSpec as P

MESH = pl.DeviceIdType.MESH
HI = lax.Precision.HIGHEST
F32 = jnp.float32

MID = lax.Precision.HIGH

def mm(a, b, ca=1, cb=0, prec=HI):
    return lax.dot_general(a, b, (((ca,), (cb,)), ((), ())), precision=prec, preferred_element_type=jnp.float32)

def inverse_factors(mats, PW=64, IB=16):
    n = 128
    lane = lax.broadcasted_iota(jnp.int32, (8, n), 1)
    sub = lax.broadcasted_iota(jnp.int32, (8, n), 0)
    nb = n // 8
    X = [[m[8 * i:8 * i + 8] for i in range(nb)] for m in mats]
    for r0 in range(0, n, PW):
        b0, b1 = r0 // 8, (r0 + PW) // 8
        D = [[None] * nb for _ in mats]
        for i0 in range(r0, r0 + PW, IB):
            ib = i0 // 8
            inner = (lane >= i0) & (lane < i0 + IB)
            CB = [[[None] * nb for _ in range(IB)] for _ in mats]
            for q in range(len(mats)):
                for k in range(IB):
                    for b in range((i0 + k) // 8, b1):
                        CB[q][k][b] = jnp.broadcast_to(X[q][b][:, i0 + k:i0 + k + 1], (8, n))
                for b in range(ib, b1):
                    X[q][b] = jnp.where(inner, jnp.where(lane == sub + 8 * b, 1.0, 0.0), X[q][b])
            for j in range(IB):
                row = i0 + j
                jb, js = row // 8, row % 8
                for q in range(len(mats)):
                    c = CB[q][j]
                    piv = jnp.broadcast_to(c[jb][js:js + 1], (8, n))
                    D[q][jb] = piv if D[q][jb] is None else jnp.where(sub >= js, piv, D[q][jb])
                    r = 1.0 / piv
                    xrow = jnp.broadcast_to(X[q][jb][js:js + 1], (8, n))
                    m = [None if b < jb or b >= b1 else c[b] * r for b in range(nb)]
                    for k in range(j + 1, IB):
                        kr = i0 + k
                        s = jnp.broadcast_to(c[kr // 8][kr % 8:kr % 8 + 1], (8, n))
                        for b in range(kr // 8, b1):
                            CB[q][k][b] = CB[q][k][b] - m[b] * s
                    for b in range(jb, b1):
                        if b == jb:
                            if js == 7: continue
                            X[q][b] = X[q][b] - jnp.where(sub > js, m[b], 0.0) * xrow
                        else:
                            X[q][b] = X[q][b] - m[b] * xrow
        for q in range(len(mats)):
            for b in range(b0, b1):
                X[q][b] = X[q][b] * lax.rsqrt(D[q][b])
                if IB < PW:
                    X[q][b] = jnp.where((lane > sub + 8 * b) & (lane < r0 + PW), 0.0, X[q][b])
            if b1 < nb:
                U = jnp.concatenate(X[q][b0:b1], axis=0)
                upd = mm(U[:, r0 + PW:], U, 0, 0) if (r0 + PW) % 128 == 0 else mm(U, U, 0, 0)
                off = b1 if upd.shape[0] == n else 0
                panel = (lane >= r0) & (lane < r0 + PW)
                for b in range(b1, nb):
                    X[q][b] = jnp.where(panel, 0.0, X[q][b]) - upd[8 * b:8 * b + 8]
    out = []
    for q in range(len(mats)):
        out.append(jnp.concatenate([jnp.where(lane <= sub + 8 * b, X[q][b], 0.0) for b in range(nb)], axis=0))
    return out

def inverse_pair(Y, PW=64, IB=16):
    n = 128
    lane = lax.broadcasted_iota(jnp.int32, (8, n), 1)
    sub = lax.broadcasted_iota(jnp.int32, (8, n), 0)
    first = lane < 64
    col = jnp.where(first, lane, lane - 64)
    nb = n // 8
    X = [[Y[8 * b:8 * b + 8, n * t:n * t + n] for b in range(nb)] for t in range(2)]
    for r0 in range(0, n, PW):
        b0, b1 = r0 // 8, (r0 + PW) // 8
        D = [None] * nb
        for i0 in range(r0, r0 + PW, IB):
            ib = i0 // 8
            CB = [[None] * nb for _ in range(IB)]
            for k in range(IB):
                t, w = (i0 + k) // 64, (i0 + k) % 64
                for b in range((i0 + k) // 8, b1):
                    CB[k][b] = jnp.where(first, jnp.broadcast_to(X[t][b][:, w:w + 1], (8, n)), jnp.broadcast_to(X[t][b][:, 64 + w:65 + w], (8, n)))
            t, w = i0 // 64, i0 % 64
            inner = (col >= w) & (col < w + IB)
            for b in range(ib, b1):
                X[t][b] = jnp.where(inner, jnp.where(col + 64 * t == sub + 8 * b, 1.0, 0.0), X[t][b])
            for j in range(IB):
                row = i0 + j
                jb, js = row // 8, row % 8
                c = CB[j]
                piv = jnp.broadcast_to(c[jb][js:js + 1], (8, n))
                D[jb] = piv if D[jb] is None else jnp.where(sub >= js, piv, D[jb])
                r = 1.0 / piv
                xrow = [jnp.broadcast_to(X[t][jb][js:js + 1], (8, n)) for t in range(2)]
                m = [None if b < jb or b >= b1 else c[b] * r for b in range(nb)]
                for k in range(j + 1, IB):
                    kr = i0 + k
                    s = jnp.broadcast_to(c[kr // 8][kr % 8:kr % 8 + 1], (8, n))
                    for b in range(kr // 8, b1):
                        CB[k][b] = CB[k][b] - m[b] * s
                for b in range(jb, b1):
                    if b == jb and js == 7: continue
                    f = jnp.where(sub > js, m[b], 0.0) if b == jb else m[b]
                    for t in range(2):
                        X[t][b] = X[t][b] - f * xrow[t]
        tp, wp = r0 // 64, r0 % 64
        for b in range(b0, b1):
            sc = lax.rsqrt(D[b])
            for t in range(2):
                X[t][b] = X[t][b] * sc
            X[tp][b] = jnp.where((col + 64 * tp > sub + 8 * b) & (col < wp + PW), 0.0, X[tp][b])
        if b1 < nb:
            U = [jnp.concatenate(X[t][b0:b1], axis=0) for t in range(2)]
            both = jnp.concatenate(U, axis=1)
            upd = [mm(U[t], both, 0, 0) if r0 + PW < 64 * t + 64 else None for t in range(2)]
            panel = (col >= wp) & (col < wp + PW)
            for b in range(b1, nb):
                u, g = upd[b // 8], 8 * (b % 8)
                for t in range(2):
                    old = jnp.where(panel, 0.0, X[t][b]) if t == tp else X[t][b]
                    X[t][b] = old - jnp.where(first, u[g:g + 8, n * t:n * t + n], u[64 + g:72 + g, n * t:n * t + n])
    for b in range(nb):
        X[b // 8][b] = jnp.where(col + 64 * (b // 8) <= sub + 8 * b, X[b // 8][b], 0.0)
        if b < 8:
            X[1][b] = jnp.zeros((8, n), jnp.float32)
    return jnp.concatenate([jnp.concatenate(X[t], axis=0) for t in range(2)], axis=1)


def doubled(rows):
    return jnp.concatenate([rows[:64], rows[:64], rows[64:], rows[64:]], axis=0)


def interleaved(rows, second):
    z = jnp.zeros((64, rows.shape[1]), jnp.float32)
    parts = [z, rows[:64], z, rows[64:]] if second else [rows[:64], z, rows[64:], z]
    return jnp.concatenate(parts, axis=0)


def k2(core_of, opts, gk, gc, stack, sketch_hbm, proj_hbm, sketch, proj, sem):
    core = core_of()
    n = 128
    Ka = gk[0:8].reshape(n, n)
    Kb = gk[8:16].reshape(n, n)
    C = gc[...].reshape(n, n)
    WT = jnp.concatenate([Ka, C], axis=1)
    N = mm(WT, WT, 1, 1)
    Z = mm(WT, jnp.concatenate([WT, jnp.concatenate([C.T, Kb], axis=1)], axis=0))
    (Finv,) = inverse_factors([N], **opts)
    VT = mm(Finv, WT)
    VG = mm(Finv, Z)
    V2 = doubled(VT)
    H = mm(VG, VT, 1, 1)
    H2 = mm(VG, V2, 1, 1)
    delta = jnp.sum(jnp.sum(VG * VT, axis=0, keepdims=True), axis=1, keepdims=True) * (1.0 / n)
    ii = lax.broadcasted_iota(jnp.int32, (n, 2 * n), 0)
    jj = lax.broadcasted_iota(jnp.int32, (n, 2 * n), 1)
    second = jj % n >= 64
    VF = interleaved(mm(VT, stack[...].reshape(2 * n, stack.shape[2])), False)
    own = jnp.where(core == 1, jnp.concatenate([C.T, Kb], axis=1), WT)
    GV = jnp.where(second, 0.0, mm(own, V2, 1, 1))
    both = inverse_pair(H2 + jnp.where(second & (ii == jj % 64 + 64 * (jj // n)), delta, 0.0), **opts)
    WF = mm(both, VF)
    PT = mm(jnp.where(second, H2, 0.0), both, 1, 1, MID)
    Pm = mm(both, interleaved(H, True), prec=MID)
    YT = mm(GV, both, 1, 1)
    sk = mm(PT, WF, prec=MID)
    sketch[...] = sk
    out = pltpu.make_async_copy(sketch, sketch_hbm, sem.at[0])
    out.start()
    co = mm(YT, Pm, prec=MID)
    gram_trace = jnp.sum(jnp.sum(Pm * Pm, axis=0, keepdims=True), axis=1, keepdims=True)
    proj[...] = mm(co * ((4.0 * n) / (gram_trace + 1e-06)), sk, prec=MID)
    last = pltpu.make_async_copy(proj, proj_hbm, sem.at[1])
    last.start()
    out.wait()
    last.wait()


def call_k2(gk, gc, stack, core_of=lambda: lax.axis_index("frames"), opts=dict(PW=64, IB=16), name="merge_project"):
    V = pl.BlockSpec(memory_space=pltpu.VMEM)
    o = jax.ShapeDtypeStruct((128, 512), jnp.float32)
    return pl.pallas_call(functools.partial(k2, core_of, opts), out_shape=[o, o], in_specs=[V] * 3, out_specs=[pl.BlockSpec(memory_space=pltpu.HBM)] * 2,
        scratch_shapes=[pltpu.VMEM((128, 512), jnp.float32)] * 2 + [pltpu.SemaphoreType.DMA((2,))],
        compiler_params=pltpu.CompilerParams(vmem_limit_bytes=32 << 20), name=name)(gk, gc, stack)


def tree(buf, own):
    v = [own] + [buf[e] for e in range(1, 8)]
    while len(v) > 1:
        v = [v[i] + v[i + 1] for i in range(0, len(v), 2)]
    return v[0]


NEAR = (7, 6, 5, 3, 4, 2, 1)


def step(e, unit):
    return unit * ((e & 1) + 4 * (e >> 1 & 1) + 16 * (e >> 2))


def k1(hbm, gk, gc, stack, kown, cown, rk, rc, sk, sc, zk, zc, s_in, s_ex, r_ex, s_rs, r_rs, s_z, r_z, s_ag, r_ag):
    core = lax.axis_index("frames")
    pix = lax.axis_index("pix")
    partner = (core + 1) % 2
    load = pltpu.make_async_copy(hbm, stack.at[core], s_in)
    load.start()
    bit = lambda t: (t % 4 + 1) // 2 % 2
    own = bit(pix) + 2 * bit(pix // 4) + 4 * bit(pix // 16)
    mates = [((core + f) % 2, pix ^ step(e, 1)) for e in NEAR + (0,) for f in (0, 1) if e or f]
    others = [(core, pix ^ step(e, 3)) for e in NEAR]
    bar = pltpu.get_barrier_semaphore()
    for device in others + mates:
        pl.semaphore_signal(bar, inc=1, device_id=device, device_id_type=MESH)

    def rcopy(src, dst, ss, rs, device):
        return pltpu.make_async_remote_copy(src_ref=src, dst_ref=dst, send_sem=ss, recv_sem=rs, device_id=device, device_id_type=MESH)

    load.wait()
    mine = stack[core]
    kown[...] = mm(mine, mine, 1, 1).reshape(8, 16, 128)
    pl.semaphore_wait(bar, len(others + mates))
    ex = rcopy(stack.at[core], stack.at[core], s_ex, r_ex, (partner, pix))
    ex.start()

    def scatter(block, into, i):
        for e in NEAR:
            rcopy(block.at[own ^ e], into.at[e], s_rs.at[i], r_rs.at[i], (core, pix ^ step(e, 1))).start()

    def across(block, into, i):
        for e in NEAR:
            rcopy(block, into.at[e], s_z.at[i], r_z.at[i], (core, pix ^ step(e, 3))).start()

    def gather(g, i):
        for device in mates:
            rcopy(g.at[core * 8 + own], g.at[core * 8 + own], s_ag.at[i], r_ag.at[i], device).start()

    def wait_for(buf, ss, rs, count):
        some = buf.at[pl.ds(0, count)]
        rcopy(some, some, ss, rs, (partner, pix)).wait()

    scatter(kown, rk, 0)
    ex.wait()
    half = pl.multiple_of(core * 64, 64)
    cown[...] = mm(stack[0, pl.ds(half, 64), :], stack[1], 1, 1).reshape(8, 8, 128)
    scatter(cown, rc, 1)
    wait_for(rk, s_rs.at[0], r_rs.at[0], 7)
    sk[...] = tree(rk, kown[own])
    across(sk, zk, 0)
    wait_for(rc, s_rs.at[1], r_rs.at[1], 7)
    sc[...] = tree(rc, cown[own])
    across(sc, zc, 1)
    wait_for(zk, s_z.at[0], r_z.at[0], 7)
    gk[core * 8 + own] = tree(zk, sk[...])
    gather(gk, 0)
    wait_for(zc, s_z.at[1], r_z.at[1], 7)
    gc[core * 8 + own] = tree(zc, sc[...])
    gather(gc, 1)
    wait_for(gk, s_ag.at[0], r_ag.at[0], 15)
    wait_for(gc, s_ag.at[1], r_ag.at[1], 15)


def call_k1(frames):
    vm = pl.BlockSpec(memory_space=pltpu.VMEM)
    dma = pltpu.SemaphoreType.DMA
    return pl.pallas_call(
        k1,
        out_shape=[
            jax.ShapeDtypeStruct((16, 16, 128), F32),
            jax.ShapeDtypeStruct((16, 8, 128), F32),
            jax.ShapeDtypeStruct((2, 128, 512), F32),
        ],
        in_specs=[pl.BlockSpec(memory_space=pltpu.HBM)],
        out_specs=[vm] * 3,
        scratch_shapes=[
            pltpu.VMEM((8, 16, 128), F32),
            pltpu.VMEM((8, 8, 128), F32),
            pltpu.VMEM((8, 16, 128), F32),
            pltpu.VMEM((8, 8, 128), F32),
            pltpu.VMEM((16, 128), F32),
            pltpu.VMEM((8, 128), F32),
            pltpu.VMEM((8, 16, 128), F32),
            pltpu.VMEM((8, 8, 128), F32),
            dma(()), dma(()), dma(()), dma((2,)), dma((2,)), dma((2,)), dma((2,)), dma((2,)), dma((2,)),
        ],
        compiler_params=pltpu.CompilerParams(collective_id=0, has_side_effects=True, vmem_limit_bytes=32 << 20),
        name="gram_exchange",
    )(frames)


def local(frames):
    gk, gc, stack = call_k1(pltpu.with_memory_space_constraint(frames, pltpu.HBM))
    return tuple(call_k2(gk, gc, stack))


def solution(mesh):
    return jax.shard_map(
        local,
        mesh=mesh,
        in_specs=(P("frames", "pix"),),
        out_specs=(P(None, "pix"), P("frames", "pix")),
        check_vma=False,
    )
```

```python
import functools
import jax
import jax.numpy as jnp
from jax import lax
from jax.experimental import pallas as pl
from jax.experimental.pallas import tpu as pltpu
from jax.sharding import PartitionSpec as P

MESH = pl.DeviceIdType.MESH
HI = lax.Precision.HIGHEST
F32 = jnp.float32

MID = lax.Precision.HIGH

def mm(a, b, ca=1, cb=0, prec=HI):
    return lax.dot_general(a, b, (((ca,), (cb,)), ((), ())), precision=prec, preferred_element_type=jnp.float32)

def inverse_factors(mats, PW=64, IB=16):
    n = 128
    lane = lax.broadcasted_iota(jnp.int32, (8, n), 1)
    sub = lax.broadcasted_iota(jnp.int32, (8, n), 0)
    nb = n // 8
    X = [[m[8 * i:8 * i + 8] for i in range(nb)] for m in mats]
    for r0 in range(0, n, PW):
        b0, b1 = r0 // 8, (r0 + PW) // 8
        D = [[None] * nb for _ in mats]
        for i0 in range(r0, r0 + PW, IB):
            ib = i0 // 8
            inner = (lane >= i0) & (lane < i0 + IB)
            CB = [[[None] * nb for _ in range(IB)] for _ in mats]
            for q in range(len(mats)):
                for near in (True, False):
                    for k in range(IB):
                        for b in range((i0 + k) // 8, b1):
                            if (b < ib + IB // 8) == near:
                                CB[q][k][b] = jnp.broadcast_to(X[q][b][:, i0 + k:i0 + k + 1], (8, n))
                for b in range(ib, b1):
                    X[q][b] = jnp.where(inner, jnp.where(lane == sub + 8 * b, 1.0, 0.0), X[q][b])
            for j in range(IB):
                row = i0 + j
                jb, js = row // 8, row % 8
                for q in range(len(mats)):
                    c = CB[q][j]
                    piv = jnp.broadcast_to(c[jb][js:js + 1], (8, n))
                    D[q][jb] = piv if D[q][jb] is None else jnp.where(sub >= js, piv, D[q][jb])
                    r = 1.0 / piv
                    xrow = jnp.broadcast_to(X[q][jb][js:js + 1], (8, n))
                    m = [None if b < jb or b >= b1 else c[b] * r for b in range(nb)]
                    for k in range(j + 1, IB):
                        kr = i0 + k
                        s = jnp.broadcast_to(c[kr // 8][kr % 8:kr % 8 + 1], (8, n))
                        for b in range(kr // 8, b1):
                            CB[q][k][b] = CB[q][k][b] - m[b] * s
                    for b in range(jb, b1):
                        if b == jb:
                            if js == 7: continue
                            X[q][b] = X[q][b] - jnp.where(sub > js, m[b], 0.0) * xrow
                        else:
                            X[q][b] = X[q][b] - m[b] * xrow
        for q in range(len(mats)):
            for b in range(b0, b1):
                X[q][b] = X[q][b] * lax.rsqrt(D[q][b])
                if IB < PW:
                    X[q][b] = jnp.where((lane > sub + 8 * b) & (lane < r0 + PW), 0.0, X[q][b])
            if b1 < nb:
                U = jnp.concatenate(X[q][b0:b1], axis=0)
                upd = mm(U[:, r0 + PW:], U, 0, 0) if (r0 + PW) % 128 == 0 else mm(U, U, 0, 0)
                off = b1 if upd.shape[0] == n else 0
                panel = (lane >= r0) & (lane < r0 + PW)
                for b in range(b1, nb):
                    X[q][b] = jnp.where(panel, 0.0, X[q][b]) - upd[8 * b:8 * b + 8]
    out = []
    for q in range(len(mats)):
        out.append(jnp.concatenate([jnp.where(lane <= sub + 8 * b, X[q][b], 0.0) for b in range(nb)], axis=0))
    return out

def inverse_pair(Y, PW=64, IB=16):
    n = 128
    lane = lax.broadcasted_iota(jnp.int32, (8, n), 1)
    sub = lax.broadcasted_iota(jnp.int32, (8, n), 0)
    first = lane < 64
    col = jnp.where(first, lane, lane - 64)
    nb = n // 8
    X = [[Y[8 * b:8 * b + 8, n * t:n * t + n] for b in range(nb)] for t in range(2)]
    for r0 in range(0, n, PW):
        b0, b1 = r0 // 8, (r0 + PW) // 8
        D = [None] * nb
        for i0 in range(r0, r0 + PW, IB):
            ib = i0 // 8
            CB = [[None] * nb for _ in range(IB)]
            for near in (True, False):
                for k in range(IB):
                    t, w = (i0 + k) // 64, (i0 + k) % 64
                    for b in range((i0 + k) // 8, b1):
                        if (b < ib + IB // 8) == near:
                            CB[k][b] = jnp.where(first, jnp.broadcast_to(X[t][b][:, w:w + 1], (8, n)), jnp.broadcast_to(X[t][b][:, 64 + w:65 + w], (8, n)))
            t, w = i0 // 64, i0 % 64
            inner = (col >= w) & (col < w + IB)
            for b in range(ib, b1):
                X[t][b] = jnp.where(inner, jnp.where(col + 64 * t == sub + 8 * b, 1.0, 0.0), X[t][b])
            for j in range(IB):
                row = i0 + j
                jb, js = row // 8, row % 8
                c = CB[j]
                piv = jnp.broadcast_to(c[jb][js:js + 1], (8, n))
                D[jb] = piv if D[jb] is None else jnp.where(sub >= js, piv, D[jb])
                r = 1.0 / piv
                xrow = [jnp.broadcast_to(X[t][jb][js:js + 1], (8, n)) for t in range(2)]
                m = [None if b < jb or b >= b1 else c[b] * r for b in range(nb)]
                for k in range(j + 1, IB):
                    kr = i0 + k
                    s = jnp.broadcast_to(c[kr // 8][kr % 8:kr % 8 + 1], (8, n))
                    for b in range(kr // 8, b1):
                        CB[k][b] = CB[k][b] - m[b] * s
                for b in range(jb, b1):
                    if b == jb and js == 7: continue
                    f = jnp.where(sub > js, m[b], 0.0) if b == jb else m[b]
                    for t in range(2):
                        X[t][b] = X[t][b] - f * xrow[t]
        tp, wp = r0 // 64, r0 % 64
        for b in range(b0, b1):
            sc = lax.rsqrt(D[b])
            for t in range(2):
                X[t][b] = X[t][b] * sc
            X[tp][b] = jnp.where((col + 64 * tp > sub + 8 * b) & (col < wp + PW), 0.0, X[tp][b])
        if b1 < nb:
            U = [jnp.concatenate(X[t][b0:b1], axis=0) for t in range(2)]
            both = jnp.concatenate(U, axis=1)
            upd = [mm(U[t], both, 0, 0) if r0 + PW < 64 * t + 64 else None for t in range(2)]
            panel = (col >= wp) & (col < wp + PW)
            for b in range(b1, nb):
                u, g = upd[b // 8], 8 * (b % 8)
                for t in range(2):
                    old = jnp.where(panel, 0.0, X[t][b]) if t == tp else X[t][b]
                    X[t][b] = old - jnp.where(first, u[g:g + 8, n * t:n * t + n], u[64 + g:72 + g, n * t:n * t + n])
    for b in range(nb):
        X[b // 8][b] = jnp.where(col + 64 * (b // 8) <= sub + 8 * b, X[b // 8][b], 0.0)
        if b < 8:
            X[1][b] = jnp.zeros((8, n), jnp.float32)
    return jnp.concatenate([jnp.concatenate(X[t], axis=0) for t in range(2)], axis=1)


def doubled(rows):
    return jnp.concatenate([rows[:64], rows[:64], rows[64:], rows[64:]], axis=0)


def interleaved(rows, second):
    z = jnp.zeros((64, rows.shape[1]), jnp.float32)
    parts = [z, rows[:64], z, rows[64:]] if second else [rows[:64], z, rows[64:], z]
    return jnp.concatenate(parts, axis=0)


def k2(core_of, opts, gk, gc, stack, sketch_hbm, proj_hbm, sketch, proj, sem):
    core = core_of()
    n = 128
    Ka = gk[0:8].reshape(n, n)
    Kb = gk[8:16].reshape(n, n)
    C = gc[...].reshape(n, n)
    WT = jnp.concatenate([Ka, C], axis=1)
    N = mm(WT, WT, 1, 1)
    Z = mm(WT, jnp.concatenate([WT, jnp.concatenate([C.T, Kb], axis=1)], axis=0))
    (Finv,) = inverse_factors([N], **opts)
    VT = mm(Finv, WT)
    VG = mm(Finv, Z)
    V2 = doubled(VT)
    H = mm(VG, VT, 1, 1)
    H2 = mm(VG, V2, 1, 1)
    delta = jnp.sum(jnp.sum(VG * VT, axis=0, keepdims=True), axis=1, keepdims=True) * (1.0 / n)
    ii = lax.broadcasted_iota(jnp.int32, (n, 2 * n), 0)
    jj = lax.broadcasted_iota(jnp.int32, (n, 2 * n), 1)
    second = jj % n >= 64
    VF = interleaved(mm(VT, stack[...].reshape(2 * n, stack.shape[2])), False)
    own = jnp.where(core == 1, jnp.concatenate([C.T, Kb], axis=1), WT)
    GV = jnp.where(second, 0.0, mm(own, V2, 1, 1))
    both = inverse_pair(H2 + jnp.where(second & (ii == jj % 64 + 64 * (jj // n)), delta, 0.0), **opts)
    WF = mm(both, VF)
    PT = mm(jnp.where(second, H2, 0.0), both, 1, 1, MID)
    Pm = mm(both, interleaved(H, True), prec=MID)
    YT = mm(GV, both, 1, 1)
    sk = mm(PT, WF, prec=MID)
    sketch[...] = sk
    out = pltpu.make_async_copy(sketch, sketch_hbm, sem.at[0])
    out.start()
    co = mm(YT, Pm, prec=MID)
    gram_trace = jnp.sum(jnp.sum(Pm * Pm, axis=0, keepdims=True), axis=1, keepdims=True)
    scaled = co * ((4.0 * n) / (gram_trace + 1e-06))
    parts = []
    for i in range(2):
        cols = pl.ds(256 * i, 256)
        proj[:, cols] = mm(scaled, sk[:, 256 * i:256 * i + 256], prec=MID)
        part = pltpu.make_async_copy(proj.at[:, cols], proj_hbm.at[:, cols], sem.at[1 + i])
        part.start()
        parts.append(part)
    out.wait()
    for part in parts:
        part.wait()


def call_k2(gk, gc, stack, core_of=lambda: lax.axis_index("frames"), opts=dict(PW=64, IB=16), name="merge_project"):
    V = pl.BlockSpec(memory_space=pltpu.VMEM)
    o = jax.ShapeDtypeStruct((128, 512), jnp.float32)
    return pl.pallas_call(functools.partial(k2, core_of, opts), out_shape=[o, o], in_specs=[V] * 3, out_specs=[pl.BlockSpec(memory_space=pltpu.HBM)] * 2,
        scratch_shapes=[pltpu.VMEM((128, 512), jnp.float32)] * 2 + [pltpu.SemaphoreType.DMA((3,))],
        compiler_params=pltpu.CompilerParams(vmem_limit_bytes=32 << 20), name=name)(gk, gc, stack)


def tree(buf, own):
    v = [own] + [buf[e] for e in range(1, 8)]
    while len(v) > 1:
        v = [v[i] + v[i + 1] for i in range(0, len(v), 2)]
    return v[0]


NEAR = (7, 6, 5, 3, 4, 2, 1)


def step(e, unit):
    return unit * ((e & 1) + 4 * (e >> 1 & 1) + 16 * (e >> 2))


def k1(hbm, gk, gc, stack, kown, cown, rk, rc, sk, sc, zk, zc, s_in, s_ex, r_ex, s_rs, r_rs, s_z, r_z, s_ag, r_ag, note):
    core = lax.axis_index("frames")
    pix = lax.axis_index("pix")
    partner = (core + 1) % 2
    load = pltpu.make_async_copy(hbm, stack.at[core], s_in)
    load.start()
    bit = lambda t: (t % 4 + 1) // 2 % 2
    own = bit(pix) + 2 * bit(pix // 4) + 4 * bit(pix // 16)
    mates = [((core + f) % 2, pix ^ step(e, 1)) for e in (0,) + NEAR for f in (1, 0) if e or f]
    across_one = [(core, pix ^ (3 * unit)) for unit in (16, 4, 1)]
    bar = pltpu.get_barrier_semaphore()
    for device in mates + across_one:
        pl.semaphore_signal(bar, inc=1, device_id=device, device_id_type=MESH)

    def rcopy(src, dst, ss, rs, device):
        return pltpu.make_async_remote_copy(src_ref=src, dst_ref=dst, send_sem=ss, recv_sem=rs, device_id=device, device_id_type=MESH)

    load.wait()
    mine = stack[core]
    kown[...] = mm(mine, mine, 1, 1).reshape(8, 16, 128)
    pl.semaphore_wait(bar, len(mates + across_one))
    ex = rcopy(stack.at[core], stack.at[core], s_ex, r_ex, (partner, pix))
    ex.start()

    def scatter(block, into, i):
        for e in NEAR:
            rcopy(block.at[own ^ e], into.at[e], s_rs.at[i], r_rs.at[i], (core, pix ^ step(e, 1))).start()

    def across(block, into, i):
        for e in NEAR:
            rcopy(block, into.at[e], s_z.at[i], r_z.at[i], (core, pix ^ step(e, 3))).start()

    def gather(g, i):
        for device in mates:
            rcopy(g.at[core * 8 + own], g.at[core * 8 + own], s_ag.at[i], r_ag.at[i], device).start()

    def wait_for(buf, ss, rs, count):
        some = buf.at[pl.ds(0, count)]
        rcopy(some, some, ss, rs, (partner, pix)).wait()

    def tell(i):
        for device in across_one:
            pl.semaphore_signal(note.at[i], inc=1, device_id=device, device_id_type=MESH)

    tell(0)
    scatter(kown, rk, 0)
    ex.wait()
    half = pl.multiple_of(core * 64, 64)
    cown[...] = mm(stack[0, pl.ds(half, 64), :], stack[1], 1, 1).reshape(8, 8, 128)
    scatter(cown, rc, 1)
    pl.semaphore_wait(note.at[0], 3)
    tell(1)
    wait_for(rk, s_rs.at[0], r_rs.at[0], 7)
    sk[...] = tree(rk, kown[own])
    pl.semaphore_wait(note.at[1], 3)
    across(sk, zk, 0)
    wait_for(rc, s_rs.at[1], r_rs.at[1], 7)
    sc[...] = tree(rc, cown[own])
    across(sc, zc, 1)
    wait_for(zk, s_z.at[0], r_z.at[0], 7)
    gk[core * 8 + own] = tree(zk, sk[...])
    gather(gk, 0)
    wait_for(zc, s_z.at[1], r_z.at[1], 7)
    gc[core * 8 + own] = tree(zc, sc[...])
    gather(gc, 1)
    wait_for(gk, s_ag.at[0], r_ag.at[0], 15)
    wait_for(gc, s_ag.at[1], r_ag.at[1], 15)


def call_k1(frames):
    vm = pl.BlockSpec(memory_space=pltpu.VMEM)
    dma = pltpu.SemaphoreType.DMA
    return pl.pallas_call(
        k1,
        out_shape=[
            jax.ShapeDtypeStruct((16, 16, 128), F32),
            jax.ShapeDtypeStruct((16, 8, 128), F32),
            jax.ShapeDtypeStruct((2, 128, 512), F32),
        ],
        in_specs=[pl.BlockSpec(memory_space=pltpu.HBM)],
        out_specs=[vm] * 3,
        scratch_shapes=[
            pltpu.VMEM((8, 16, 128), F32),
            pltpu.VMEM((8, 8, 128), F32),
            pltpu.VMEM((8, 16, 128), F32),
            pltpu.VMEM((8, 8, 128), F32),
            pltpu.VMEM((16, 128), F32),
            pltpu.VMEM((8, 128), F32),
            pltpu.VMEM((8, 16, 128), F32),
            pltpu.VMEM((8, 8, 128), F32),
            dma(()), dma(()), dma(()), dma((2,)), dma((2,)), dma((2,)), dma((2,)), dma((2,)), dma((2,)),
            pltpu.SemaphoreType.REGULAR((2,)),
        ],
        compiler_params=pltpu.CompilerParams(collective_id=0, has_side_effects=True, vmem_limit_bytes=32 << 20),
        name="gram_exchange",
    )(frames)


def local(frames):
    gk, gc, stack = call_k1(pltpu.with_memory_space_constraint(frames, pltpu.HBM))
    return tuple(call_k2(gk, gc, stack))


def solution(mesh):
    return jax.shard_map(
        local,
        mesh=mesh,
        in_specs=(P("frames", "pix"),),
        out_specs=(P(None, "pix"), P("frames", "pix")),
        check_vma=False,
    )
```

```python
import functools
import jax
import jax.numpy as jnp
from jax import lax
from jax.experimental import pallas as pl
from jax.experimental.pallas import tpu as pltpu
from jax.sharding import PartitionSpec as P

MESH = pl.DeviceIdType.MESH
HI = lax.Precision.HIGHEST
F32 = jnp.float32

MID = lax.Precision.HIGH

def mm(a, b, ca=1, cb=0, prec=HI):
    return lax.dot_general(a, b, (((ca,), (cb,)), ((), ())), precision=prec, preferred_element_type=jnp.float32)

def inverse_factors(mats, PW=64, IB=16):
    n = 128
    lane = lax.broadcasted_iota(jnp.int32, (8, n), 1)
    sub = lax.broadcasted_iota(jnp.int32, (8, n), 0)
    nb = n // 8
    X = [[m[8 * i:8 * i + 8] for i in range(nb)] for m in mats]
    for r0 in range(0, n, PW):
        b0, b1 = r0 // 8, (r0 + PW) // 8
        D = [[None] * nb for _ in mats]
        for i0 in range(r0, r0 + PW, IB):
            ib = i0 // 8
            inner = (lane >= i0) & (lane < i0 + IB)
            CB = [[[None] * nb for _ in range(IB)] for _ in mats]
            for q in range(len(mats)):
                for near in (True, False):
                    for k in range(IB):
                        for b in range((i0 + k) // 8, b1):
                            if (b < ib + IB // 8) == near:
                                CB[q][k][b] = jnp.broadcast_to(X[q][b][:, i0 + k:i0 + k + 1], (8, n))
                for b in range(ib, b1):
                    X[q][b] = jnp.where(inner, jnp.where(lane == sub + 8 * b, 1.0, 0.0), X[q][b])
            for j in range(IB):
                row = i0 + j
                jb, js = row // 8, row % 8
                for q in range(len(mats)):
                    c = CB[q][j]
                    piv = jnp.broadcast_to(c[jb][js:js + 1], (8, n))
                    D[q][jb] = piv if D[q][jb] is None else jnp.where(sub >= js, piv, D[q][jb])
                    r = 1.0 / piv
                    xrow = jnp.broadcast_to(X[q][jb][js:js + 1], (8, n))
                    m = [None if b < jb or b >= b1 else c[b] * r for b in range(nb)]
                    for k in range(j + 1, IB):
                        kr = i0 + k
                        s = jnp.broadcast_to(c[kr // 8][kr % 8:kr % 8 + 1], (8, n))
                        for b in range(kr // 8, b1):
                            CB[q][k][b] = CB[q][k][b] - m[b] * s
                    for b in range(jb, b1):
                        if b == jb:
                            if js == 7: continue
                            X[q][b] = X[q][b] - jnp.where(sub > js, m[b], 0.0) * xrow
                        else:
                            X[q][b] = X[q][b] - m[b] * xrow
        for q in range(len(mats)):
            for b in range(b0, b1):
                X[q][b] = X[q][b] * lax.rsqrt(D[q][b])
                if IB < PW:
                    X[q][b] = jnp.where((lane > sub + 8 * b) & (lane < r0 + PW), 0.0, X[q][b])
            if b1 < nb:
                U = jnp.concatenate(X[q][b0:b1], axis=0)
                upd = mm(U[:, r0 + PW:], U, 0, 0) if (r0 + PW) % 128 == 0 else mm(U, U, 0, 0)
                off = b1 if upd.shape[0] == n else 0
                panel = (lane >= r0) & (lane < r0 + PW)
                for b in range(b1, nb):
                    X[q][b] = jnp.where(panel, 0.0, X[q][b]) - upd[8 * b:8 * b + 8]
    out = []
    for q in range(len(mats)):
        out.append(jnp.concatenate([jnp.where(lane <= sub + 8 * b, X[q][b], 0.0) for b in range(nb)], axis=0))
    return out

def inverse_pair(Y, PW=64, IB=16):
    n = 128
    lane = lax.broadcasted_iota(jnp.int32, (8, n), 1)
    sub = lax.broadcasted_iota(jnp.int32, (8, n), 0)
    first = lane < 64
    col = jnp.where(first, lane, lane - 64)
    nb = n // 8
    X = [[Y[8 * b:8 * b + 8, n * t:n * t + n] for b in range(nb)] for t in range(2)]
    for r0 in range(0, n, PW):
        b0, b1 = r0 // 8, (r0 + PW) // 8
        D = [None] * nb
        for i0 in range(r0, r0 + PW, IB):
            ib = i0 // 8
            CB = [[None] * nb for _ in range(IB)]
            for near in (True, False):
                for k in range(IB):
                    t, w = (i0 + k) // 64, (i0 + k) % 64
                    for b in range((i0 + k) // 8, b1):
                        if (b < ib + IB // 8) == near:
                            CB[k][b] = jnp.where(first, jnp.broadcast_to(X[t][b][:, w:w + 1], (8, n)), jnp.broadcast_to(X[t][b][:, 64 + w:65 + w], (8, n)))
            t, w = i0 // 64, i0 % 64
            inner = (col >= w) & (col < w + IB)
            for b in range(ib, b1):
                X[t][b] = jnp.where(inner, jnp.where(col + 64 * t == sub + 8 * b, 1.0, 0.0), X[t][b])
            for j in range(IB):
                row = i0 + j
                jb, js = row // 8, row % 8
                c = CB[j]
                piv = jnp.broadcast_to(c[jb][js:js + 1], (8, n))
                D[jb] = piv if D[jb] is None else jnp.where(sub >= js, piv, D[jb])
                r = 1.0 / piv
                xrow = [jnp.broadcast_to(X[t][jb][js:js + 1], (8, n)) for t in range(2)]
                m = [None if b < jb or b >= b1 else c[b] * r for b in range(nb)]
                for k in range(j + 1, IB):
                    kr = i0 + k
                    s = jnp.broadcast_to(c[kr // 8][kr % 8:kr % 8 + 1], (8, n))
                    for b in range(kr // 8, b1):
                        CB[k][b] = CB[k][b] - m[b] * s
                for b in range(jb, b1):
                    if b == jb and js == 7: continue
                    f = jnp.where(sub > js, m[b], 0.0) if b == jb else m[b]
                    for t in range(2):
                        X[t][b] = X[t][b] - f * xrow[t]
        tp, wp = r0 // 64, r0 % 64
        for b in range(b0, b1):
            sc = lax.rsqrt(D[b])
            for t in range(2):
                X[t][b] = X[t][b] * sc
            X[tp][b] = jnp.where((col + 64 * tp > sub + 8 * b) & (col < wp + PW), 0.0, X[tp][b])
        if b1 < nb:
            U = [jnp.concatenate(X[t][b0:b1], axis=0) for t in range(2)]
            both = jnp.concatenate(U, axis=1)
            upd = [mm(U[t], both, 0, 0) if r0 + PW < 64 * t + 64 else None for t in range(2)]
            panel = (col >= wp) & (col < wp + PW)
            for b in range(b1, nb):
                u, g = upd[b // 8], 8 * (b % 8)
                for t in range(2):
                    old = jnp.where(panel, 0.0, X[t][b]) if t == tp else X[t][b]
                    X[t][b] = old - jnp.where(first, u[g:g + 8, n * t:n * t + n], u[64 + g:72 + g, n * t:n * t + n])
    for b in range(nb):
        X[b // 8][b] = jnp.where(col + 64 * (b // 8) <= sub + 8 * b, X[b // 8][b], 0.0)
        if b < 8:
            X[1][b] = jnp.zeros((8, n), jnp.float32)
    return jnp.concatenate([jnp.concatenate(X[t], axis=0) for t in range(2)], axis=1)


def doubled(rows):
    return jnp.concatenate([rows[:64], rows[:64], rows[64:], rows[64:]], axis=0)


def interleaved(rows, second):
    z = jnp.zeros((64, rows.shape[1]), jnp.float32)
    parts = [z, rows[:64], z, rows[64:]] if second else [rows[:64], z, rows[64:], z]
    return jnp.concatenate(parts, axis=0)


def k2(core_of, opts, gk, gc, stack, sketch_hbm, proj_hbm, sketch, proj, sem):
    core = core_of()
    n = 128
    Ka = gk[0:8].reshape(n, n)
    Kb = gk[8:16].reshape(n, n)
    C = gc[...].reshape(n, n)
    WT = jnp.concatenate([Ka, C], axis=1)
    N = mm(WT, WT, 1, 1)
    Z = mm(WT, jnp.concatenate([WT, jnp.concatenate([C.T, Kb], axis=1)], axis=0))
    (Finv,) = inverse_factors([N], **opts)
    VT = mm(Finv, WT)
    VG = mm(Finv, Z)
    V2 = doubled(VT)
    H = mm(VG, VT, 1, 1)
    H2 = mm(VG, V2, 1, 1)
    delta = jnp.sum(jnp.sum(VG * VT, axis=0, keepdims=True), axis=1, keepdims=True) * (1.0 / n)
    ii = lax.broadcasted_iota(jnp.int32, (n, 2 * n), 0)
    jj = lax.broadcasted_iota(jnp.int32, (n, 2 * n), 1)
    second = jj % n >= 64
    VF = interleaved(mm(VT, stack[...].reshape(2 * n, stack.shape[2])), False)
    own = jnp.where(core == 1, jnp.concatenate([C.T, Kb], axis=1), WT)
    GV = jnp.where(second, 0.0, mm(own, V2, 1, 1))
    both = inverse_pair(H2 + jnp.where(second & (ii == jj % 64 + 64 * (jj // n)), delta, 0.0), **opts)
    WF = mm(both, VF)
    PT = mm(jnp.where(second, H2, 0.0), both, 1, 1, MID)
    Pm = mm(both, interleaved(H, True), prec=MID)
    YT = mm(GV, both, 1, 1)
    sk = mm(PT, WF, prec=MID)
    sketch[...] = sk
    out = pltpu.make_async_copy(sketch, sketch_hbm, sem.at[0])
    out.start()
    co = mm(YT, Pm, prec=MID)
    gram_trace = jnp.sum(jnp.sum(Pm * Pm, axis=0, keepdims=True), axis=1, keepdims=True)
    scaled = co * ((4.0 * n) / (gram_trace + 1e-06))
    parts = []
    for i in range(2):
        cols = pl.ds(256 * i, 256)
        proj[:, cols] = mm(scaled, sk[:, 256 * i:256 * i + 256], prec=MID)
        part = pltpu.make_async_copy(proj.at[:, cols], proj_hbm.at[:, cols], sem.at[1 + i])
        part.start()
        parts.append(part)
    out.wait()
    for part in parts:
        part.wait()


def call_k2(gk, gc, stack, core_of=lambda: lax.axis_index("frames"), opts=dict(PW=64, IB=16), name="merge_project"):
    V = pl.BlockSpec(memory_space=pltpu.VMEM)
    o = jax.ShapeDtypeStruct((128, 512), jnp.float32)
    return pl.pallas_call(functools.partial(k2, core_of, opts), out_shape=[o, o], in_specs=[V] * 3, out_specs=[pl.BlockSpec(memory_space=pltpu.HBM)] * 2,
        scratch_shapes=[pltpu.VMEM((128, 512), jnp.float32)] * 2 + [pltpu.SemaphoreType.DMA((3,))],
        compiler_params=pltpu.CompilerParams(vmem_limit_bytes=32 << 20), name=name)(gk, gc, stack)


def tree(buf, own):
    v = [own] + [buf[e] for e in range(1, 8)]
    while len(v) > 1:
        v = [v[i] + v[i + 1] for i in range(0, len(v), 2)]
    return v[0]


NEAR = (7, 6, 5, 3, 4, 2, 1)


def step(e, unit):
    return unit * ((e & 1) + 4 * (e >> 1 & 1) + 16 * (e >> 2))


def k1(hbm, gk, gc, stack, kown, cown, rk, rc, sk, sc, zk, zc, s_in, s_ex, r_ex, s_rs, r_rs, s_z, r_z, s_ag, r_ag, note):
    core = lax.axis_index("frames")
    pix = lax.axis_index("pix")
    partner = (core + 1) % 2
    load = pltpu.make_async_copy(hbm, stack.at[core], s_in)
    load.start()
    bit = lambda t: (t % 4 + 1) // 2 % 2
    own = bit(pix) + 2 * bit(pix // 4) + 4 * bit(pix // 16)
    mates = [((core + f) % 2, pix ^ step(e, 1)) for e in (0,) + NEAR for f in (1, 0) if e or f]
    across_one = [(core, pix ^ (3 * unit)) for unit in (16, 4, 1)]
    bar = pltpu.get_barrier_semaphore()
    greeted = [(partner, pix)] + [(core, pix ^ step(e, 1)) for e in NEAR] + across_one
    for device in greeted:
        pl.semaphore_signal(bar, inc=1, device_id=device, device_id_type=MESH)

    def rcopy(src, dst, ss, rs, device):
        return pltpu.make_async_remote_copy(src_ref=src, dst_ref=dst, send_sem=ss, recv_sem=rs, device_id=device, device_id_type=MESH)

    load.wait()
    mine = stack[core]
    kown[...] = mm(mine, mine, 1, 1).reshape(8, 16, 128)
    pl.semaphore_wait(bar, len(greeted))
    ex = rcopy(stack.at[core], stack.at[core], s_ex, r_ex, (partner, pix))
    ex.start()

    def scatter(block, into, i):
        for e in NEAR:
            rcopy(block.at[own ^ e], into.at[e], s_rs.at[i], r_rs.at[i], (core, pix ^ step(e, 1))).start()

    def across(block, into, i):
        for e in NEAR:
            rcopy(block, into.at[e], s_z.at[i], r_z.at[i], (core, pix ^ step(e, 3))).start()

    def gather(g, i):
        for device in mates:
            rcopy(g.at[core * 8 + own], g.at[core * 8 + own], s_ag.at[i], r_ag.at[i], device).start()

    sent = []

    def wait_for(buf, ss, rs, count):
        some = buf.at[pl.ds(0, count)]
        copy = rcopy(some, some, ss, rs, (partner, pix))
        copy.wait_recv()
        sent.append(copy)

    def tell(i):
        for device in across_one:
            pl.semaphore_signal(note.at[i], inc=1, device_id=device, device_id_type=MESH)

    tell(0)
    scatter(kown, rk, 0)
    ex.wait()
    half = pl.multiple_of(core * 64, 64)
    cown[...] = mm(stack[0, pl.ds(half, 64), :], stack[1], 1, 1).reshape(8, 8, 128)
    scatter(cown, rc, 1)
    pl.semaphore_wait(note.at[0], 3)
    tell(1)
    wait_for(rk, s_rs.at[0], r_rs.at[0], 7)
    sk[...] = tree(rk, kown[own])
    pl.semaphore_wait(note.at[1], 3)
    across(sk, zk, 0)
    wait_for(rc, s_rs.at[1], r_rs.at[1], 7)
    sc[...] = tree(rc, cown[own])
    across(sc, zc, 1)
    wait_for(zk, s_z.at[0], r_z.at[0], 7)
    gk[core * 8 + own] = tree(zk, sk[...])
    gather(gk, 0)
    wait_for(zc, s_z.at[1], r_z.at[1], 7)
    gc[core * 8 + own] = tree(zc, sc[...])
    gather(gc, 1)
    wait_for(gk, s_ag.at[0], r_ag.at[0], 15)
    wait_for(gc, s_ag.at[1], r_ag.at[1], 15)
    for copy in sent:
        copy.wait_send()


def call_k1(frames):
    vm = pl.BlockSpec(memory_space=pltpu.VMEM)
    dma = pltpu.SemaphoreType.DMA
    return pl.pallas_call(
        k1,
        out_shape=[
            jax.ShapeDtypeStruct((16, 16, 128), F32),
            jax.ShapeDtypeStruct((16, 8, 128), F32),
            jax.ShapeDtypeStruct((2, 128, 512), F32),
        ],
        in_specs=[pl.BlockSpec(memory_space=pltpu.HBM)],
        out_specs=[vm] * 3,
        scratch_shapes=[
            pltpu.VMEM((8, 16, 128), F32),
            pltpu.VMEM((8, 8, 128), F32),
            pltpu.VMEM((8, 16, 128), F32),
            pltpu.VMEM((8, 8, 128), F32),
            pltpu.VMEM((16, 128), F32),
            pltpu.VMEM((8, 128), F32),
            pltpu.VMEM((8, 16, 128), F32),
            pltpu.VMEM((8, 8, 128), F32),
            dma(()), dma(()), dma(()), dma((2,)), dma((2,)), dma((2,)), dma((2,)), dma((2,)), dma((2,)),
            pltpu.SemaphoreType.REGULAR((2,)),
        ],
        compiler_params=pltpu.CompilerParams(collective_id=0, has_side_effects=True, vmem_limit_bytes=32 << 20),
        name="gram_exchange",
    )(frames)


def local(frames):
    gk, gc, stack = call_k1(pltpu.with_memory_space_constraint(frames, pltpu.HBM))
    return tuple(call_k2(gk, gc, stack))


def solution(mesh):
    return jax.shard_map(
        local,
        mesh=mesh,
        in_specs=(P("frames", "pix"),),
        out_specs=(P(None, "pix"), P("frames", "pix")),
        check_vma=False,
    )
```

```python
import functools
import jax
import jax.numpy as jnp
from jax import lax
from jax.experimental import pallas as pl
from jax.experimental.pallas import tpu as pltpu
from jax.sharding import PartitionSpec as P

MESH = pl.DeviceIdType.MESH
HI = lax.Precision.HIGHEST
F32 = jnp.float32

MID = lax.Precision.HIGH

def mm(a, b, ca=1, cb=0, prec=HI):
    return lax.dot_general(a, b, (((ca,), (cb,)), ((), ())), precision=prec, preferred_element_type=jnp.float32)

def inverse_factors(mats, PW=64, IB=16):
    n = 128
    lane = lax.broadcasted_iota(jnp.int32, (8, n), 1)
    sub = lax.broadcasted_iota(jnp.int32, (8, n), 0)
    nb = n // 8
    X = [[m[8 * i:8 * i + 8] for i in range(nb)] for m in mats]
    for r0 in range(0, n, PW):
        b0, b1 = r0 // 8, (r0 + PW) // 8
        D = [[None] * nb for _ in mats]
        for i0 in range(r0, r0 + PW, IB):
            ib = i0 // 8
            inner = (lane >= i0) & (lane < i0 + IB)
            CB = [[[None] * nb for _ in range(IB)] for _ in mats]
            for q in range(len(mats)):
                for near in (True, False):
                    for k in range(IB):
                        for b in range((i0 + k) // 8, b1):
                            if (b < ib + IB // 8) == near:
                                CB[q][k][b] = jnp.broadcast_to(X[q][b][:, i0 + k:i0 + k + 1], (8, n))
                for b in range(ib, b1):
                    X[q][b] = jnp.where(inner, jnp.where(lane == sub + 8 * b, 1.0, 0.0), X[q][b])
            for j in range(IB):
                row = i0 + j
                jb, js = row // 8, row % 8
                for q in range(len(mats)):
                    c = CB[q][j]
                    piv = jnp.broadcast_to(c[jb][js:js + 1], (8, n))
                    D[q][jb] = piv if D[q][jb] is None else jnp.where(sub >= js, piv, D[q][jb])
                    r = 1.0 / piv
                    xrow = jnp.broadcast_to(X[q][jb][js:js + 1], (8, n))
                    m = [None if b < jb or b >= b1 else c[b] * r for b in range(nb)]
                    for k in range(j + 1, IB):
                        kr = i0 + k
                        s = jnp.broadcast_to(c[kr // 8][kr % 8:kr % 8 + 1], (8, n))
                        for b in range(kr // 8, b1):
                            CB[q][k][b] = CB[q][k][b] - m[b] * s
                    for b in range(jb, b1):
                        if b == jb:
                            if js == 7: continue
                            X[q][b] = X[q][b] - jnp.where(sub > js, m[b], 0.0) * xrow
                        else:
                            X[q][b] = X[q][b] - m[b] * xrow
        for q in range(len(mats)):
            for b in range(b0, b1):
                X[q][b] = X[q][b] * lax.rsqrt(D[q][b])
                if IB < PW:
                    X[q][b] = jnp.where((lane > sub + 8 * b) & (lane < r0 + PW), 0.0, X[q][b])
            if b1 < nb:
                U = jnp.concatenate(X[q][b0:b1], axis=0)
                upd = mm(U[:, r0 + PW:], U, 0, 0) if (r0 + PW) % 128 == 0 else mm(U, U, 0, 0)
                off = b1 if upd.shape[0] == n else 0
                panel = (lane >= r0) & (lane < r0 + PW)
                for b in range(b1, nb):
                    X[q][b] = jnp.where(panel, 0.0, X[q][b]) - upd[8 * b:8 * b + 8]
    out = []
    for q in range(len(mats)):
        out.append(jnp.concatenate([jnp.where(lane <= sub + 8 * b, X[q][b], 0.0) for b in range(nb)], axis=0))
    return out

def inverse_pair(Y, PW=64, IB=16):
    n = 128
    lane = lax.broadcasted_iota(jnp.int32, (8, n), 1)
    sub = lax.broadcasted_iota(jnp.int32, (8, n), 0)
    first = lane < 64
    col = jnp.where(first, lane, lane - 64)
    nb = n // 8
    X = [[Y[8 * b:8 * b + 8, n * t:n * t + n] for b in range(nb)] for t in range(2)]
    for r0 in range(0, n, PW):
        b0, b1 = r0 // 8, (r0 + PW) // 8
        D = [None] * nb
        for i0 in range(r0, r0 + PW, IB):
            ib = i0 // 8
            CB = [[None] * nb for _ in range(IB)]
            for near in (True, False):
                for k in range(IB):
                    t, w = (i0 + k) // 64, (i0 + k) % 64
                    for b in range((i0 + k) // 8, b1):
                        if (b < ib + IB // 8) == near:
                            CB[k][b] = jnp.where(first, jnp.broadcast_to(X[t][b][:, w:w + 1], (8, n)), jnp.broadcast_to(X[t][b][:, 64 + w:65 + w], (8, n)))
            t, w = i0 // 64, i0 % 64
            inner = (col >= w) & (col < w + IB)
            for b in range(ib, b1):
                X[t][b] = jnp.where(inner, jnp.where(col + 64 * t == sub + 8 * b, 1.0, 0.0), X[t][b])
            for j in range(IB):
                row = i0 + j
                jb, js = row // 8, row % 8
                c = CB[j]
                piv = jnp.broadcast_to(c[jb][js:js + 1], (8, n))
                D[jb] = piv if D[jb] is None else jnp.where(sub >= js, piv, D[jb])
                r = 1.0 / piv
                xrow = [jnp.broadcast_to(X[t][jb][js:js + 1], (8, n)) for t in range(2)]
                m = [None if b < jb or b >= b1 else c[b] * r for b in range(nb)]
                for k in range(j + 1, IB):
                    kr = i0 + k
                    s = jnp.broadcast_to(c[kr // 8][kr % 8:kr % 8 + 1], (8, n))
                    for b in range(kr // 8, b1):
                        CB[k][b] = CB[k][b] - m[b] * s
                for b in range(jb, b1):
                    if b == jb and js == 7: continue
                    f = jnp.where(sub > js, m[b], 0.0) if b == jb else m[b]
                    for t in range(2):
                        X[t][b] = X[t][b] - f * xrow[t]
        tp, wp = r0 // 64, r0 % 64
        for b in range(b0, b1):
            sc = lax.rsqrt(D[b])
            for t in range(2):
                X[t][b] = X[t][b] * sc
            X[tp][b] = jnp.where((col + 64 * tp > sub + 8 * b) & (col < wp + PW), 0.0, X[tp][b])
        if b1 < nb:
            U = [jnp.concatenate(X[t][b0:b1], axis=0) for t in range(2)]
            both = jnp.concatenate(U, axis=1)
            upd = [mm(U[t], both, 0, 0) if r0 + PW < 64 * t + 64 else None for t in range(2)]
            panel = (col >= wp) & (col < wp + PW)
            for b in range(b1, nb):
                u, g = upd[b // 8], 8 * (b % 8)
                for t in range(2):
                    old = jnp.where(panel, 0.0, X[t][b]) if t == tp else X[t][b]
                    X[t][b] = old - jnp.where(first, u[g:g + 8, n * t:n * t + n], u[64 + g:72 + g, n * t:n * t + n])
    for b in range(nb):
        X[b // 8][b] = jnp.where(col + 64 * (b // 8) <= sub + 8 * b, X[b // 8][b], 0.0)
        if b < 8:
            X[1][b] = jnp.zeros((8, n), jnp.float32)
    return jnp.concatenate([jnp.concatenate(X[t], axis=0) for t in range(2)], axis=1)


def doubled(rows):
    return jnp.concatenate([rows[:64], rows[:64], rows[64:], rows[64:]], axis=0)


def interleaved(rows, second):
    z = jnp.zeros((64, rows.shape[1]), jnp.float32)
    parts = [z, rows[:64], z, rows[64:]] if second else [rows[:64], z, rows[64:], z]
    return jnp.concatenate(parts, axis=0)


def k2(core_of, opts, gk, gc, stack, sketch_hbm, proj_hbm, sketch, proj, sem):
    core = core_of()
    n = 128
    Ka = gk[0:8].reshape(n, n)
    Kb = gk[8:16].reshape(n, n)
    C = gc[...].reshape(n, n)
    WT = jnp.concatenate([Ka, C], axis=1)
    N = mm(WT, WT, 1, 1)
    Z = mm(WT, jnp.concatenate([WT, jnp.concatenate([C.T, Kb], axis=1)], axis=0))
    (Finv,) = inverse_factors([N], **opts)
    VT = mm(Finv, WT)
    VG = mm(Finv, Z)
    V2 = doubled(VT)
    H = mm(VG, VT, 1, 1)
    H2 = mm(VG, V2, 1, 1)
    delta = jnp.sum(jnp.sum(VG * VT, axis=0, keepdims=True), axis=1, keepdims=True) * (1.0 / n)
    ii = lax.broadcasted_iota(jnp.int32, (n, 2 * n), 0)
    jj = lax.broadcasted_iota(jnp.int32, (n, 2 * n), 1)
    second = jj % n >= 64
    VF = interleaved(mm(VT, stack[...].reshape(2 * n, stack.shape[2])), False)
    own = jnp.where(core == 1, jnp.concatenate([C.T, Kb], axis=1), WT)
    GV = jnp.where(second, 0.0, mm(own, V2, 1, 1))
    both = inverse_pair(H2 + jnp.where(second & (ii == jj % 64 + 64 * (jj // n)), delta, 0.0), **opts)
    WF = mm(both, VF)
    PT = mm(jnp.where(second, H2, 0.0), both, 1, 1, MID)
    Pm = mm(both, interleaved(H, True), prec=MID)
    YT = mm(GV, both, 1, 1)
    sk = mm(PT, WF, prec=MID)
    sketch[...] = sk
    out = pltpu.make_async_copy(sketch, sketch_hbm, sem.at[0])
    out.start()
    co = mm(YT, Pm, prec=MID)
    gram_trace = jnp.sum(jnp.sum(Pm * Pm, axis=0, keepdims=True), axis=1, keepdims=True)
    scaled = co * ((4.0 * n) / (gram_trace + 1e-06))
    parts = []
    for i in range(2):
        cols = pl.ds(256 * i, 256)
        proj[:, cols] = mm(scaled, sk[:, 256 * i:256 * i + 256], prec=MID)
        part = pltpu.make_async_copy(proj.at[:, cols], proj_hbm.at[:, cols], sem.at[1 + i])
        part.start()
        parts.append(part)
    out.wait()
    for part in parts:
        part.wait()


def call_k2(gk, gc, stack, core_of=lambda: lax.axis_index("frames"), opts=dict(PW=64, IB=16), name="merge_project"):
    V = pl.BlockSpec(memory_space=pltpu.VMEM)
    o = jax.ShapeDtypeStruct((128, 512), jnp.float32)
    return pl.pallas_call(functools.partial(k2, core_of, opts), out_shape=[o, o], in_specs=[V] * 3, out_specs=[pl.BlockSpec(memory_space=pltpu.HBM)] * 2,
        scratch_shapes=[pltpu.VMEM((128, 512), jnp.float32)] * 2 + [pltpu.SemaphoreType.DMA((3,))],
        compiler_params=pltpu.CompilerParams(vmem_limit_bytes=32 << 20), name=name)(gk, gc, stack)


def tree(buf, own):
    v = [own] + [buf[e] for e in range(1, 8)]
    while len(v) > 1:
        v = [v[i] + v[i + 1] for i in range(0, len(v), 2)]
    return v[0]


NEAR = (7, 6, 5, 3, 4, 2, 1)


def step(e, unit):
    return unit * ((e & 1) + 4 * (e >> 1 & 1) + 16 * (e >> 2))


def k1(hbm, gk, gc, stack, kown, cown, rk, rc, sk, sc, zk, zc, s_in, s_ex, r_ex, s_rs, r_rs, s_z, r_z, s_ag, r_ag, note):
    core = lax.axis_index("frames")
    pix = lax.axis_index("pix")
    partner = (core + 1) % 2
    load = pltpu.make_async_copy(hbm, stack.at[core], s_in)
    load.start()
    bit = lambda t: (t % 4 + 1) // 2 % 2
    own = bit(pix) + 2 * bit(pix // 4) + 4 * bit(pix // 16)
    mates = [((core + f) % 2, pix ^ step(e, 1)) for e in (0,) + NEAR for f in (1, 0) if e or f]
    across_one = [(core, pix ^ (3 * unit)) for unit in (16, 4, 1)]
    bar = pltpu.get_barrier_semaphore()
    greeted = [(partner, pix)] + [(core, pix ^ step(e, 1)) for e in NEAR] + across_one
    for device in greeted:
        pl.semaphore_signal(bar, inc=1, device_id=device, device_id_type=MESH)

    def rcopy(src, dst, ss, rs, device):
        return pltpu.make_async_remote_copy(src_ref=src, dst_ref=dst, send_sem=ss, recv_sem=rs, device_id=device, device_id_type=MESH)

    load.wait()
    pl.semaphore_wait(bar, len(greeted))
    ex = rcopy(stack.at[core], stack.at[core], s_ex, r_ex, (partner, pix))
    ex.start()
    mine = stack[core]
    kown[...] = mm(mine, mine, 1, 1).reshape(8, 16, 128)

    def scatter(block, into, i):
        for e in NEAR:
            rcopy(block.at[own ^ e], into.at[e], s_rs.at[i], r_rs.at[i], (core, pix ^ step(e, 1))).start()

    def across(block, into, i):
        for e in NEAR:
            rcopy(block, into.at[e], s_z.at[i], r_z.at[i], (core, pix ^ step(e, 3))).start()

    def gather(g, i):
        for device in mates:
            rcopy(g.at[core * 8 + own], g.at[core * 8 + own], s_ag.at[i], r_ag.at[i], device).start()

    sent = []

    def wait_for(buf, ss, rs, count):
        some = buf.at[pl.ds(0, count)]
        copy = rcopy(some, some, ss, rs, (partner, pix))
        copy.wait_recv()
        sent.append(copy)

    def tell(i):
        for device in across_one:
            pl.semaphore_signal(note.at[i], inc=1, device_id=device, device_id_type=MESH)

    tell(0)
    scatter(kown, rk, 0)
    ex.wait()
    half = pl.multiple_of(core * 64, 64)
    cown[...] = mm(stack[0, pl.ds(half, 64), :], stack[1], 1, 1).reshape(8, 8, 128)
    scatter(cown, rc, 1)
    pl.semaphore_wait(note.at[0], 3)
    tell(1)
    wait_for(rk, s_rs.at[0], r_rs.at[0], 7)
    sk[...] = tree(rk, kown[own])
    pl.semaphore_wait(note.at[1], 3)
    across(sk, zk, 0)
    wait_for(rc, s_rs.at[1], r_rs.at[1], 7)
    sc[...] = tree(rc, cown[own])
    across(sc, zc, 1)
    wait_for(zk, s_z.at[0], r_z.at[0], 7)
    gk[core * 8 + own] = tree(zk, sk[...])
    gather(gk, 0)
    wait_for(zc, s_z.at[1], r_z.at[1], 7)
    gc[core * 8 + own] = tree(zc, sc[...])
    gather(gc, 1)
    wait_for(gk, s_ag.at[0], r_ag.at[0], 15)
    wait_for(gc, s_ag.at[1], r_ag.at[1], 15)
    for copy in sent:
        copy.wait_send()


def call_k1(frames):
    vm = pl.BlockSpec(memory_space=pltpu.VMEM)
    dma = pltpu.SemaphoreType.DMA
    return pl.pallas_call(
        k1,
        out_shape=[
            jax.ShapeDtypeStruct((16, 16, 128), F32),
            jax.ShapeDtypeStruct((16, 8, 128), F32),
            jax.ShapeDtypeStruct((2, 128, 512), F32),
        ],
        in_specs=[pl.BlockSpec(memory_space=pltpu.HBM)],
        out_specs=[vm] * 3,
        scratch_shapes=[
            pltpu.VMEM((8, 16, 128), F32),
            pltpu.VMEM((8, 8, 128), F32),
            pltpu.VMEM((8, 16, 128), F32),
            pltpu.VMEM((8, 8, 128), F32),
            pltpu.VMEM((16, 128), F32),
            pltpu.VMEM((8, 128), F32),
            pltpu.VMEM((8, 16, 128), F32),
            pltpu.VMEM((8, 8, 128), F32),
            dma(()), dma(()), dma(()), dma((2,)), dma((2,)), dma((2,)), dma((2,)), dma((2,)), dma((2,)),
            pltpu.SemaphoreType.REGULAR((2,)),
        ],
        compiler_params=pltpu.CompilerParams(collective_id=0, has_side_effects=True, vmem_limit_bytes=32 << 20),
        name="gram_exchange",
    )(frames)


def local(frames):
    gk, gc, stack = call_k1(pltpu.with_memory_space_constraint(frames, pltpu.HBM))
    return tuple(call_k2(gk, gc, stack))


def solution(mesh):
    return jax.shard_map(
        local,
        mesh=mesh,
        in_specs=(P("frames", "pix"),),
        out_specs=(P(None, "pix"), P("frames", "pix")),
        check_vma=False,
    )
```
